128 devices in a mesh: role: 2 (over y_lo), dev: 64 (over z, y_hi, x, core).
Axes of the slice: x: 4, y: 4 (y_hi: 2, y_lo: 2; y = y_hi * 2 + y_lo), z: 4, core: 2. Of those that a mesh axis runs over, the one named last changes fastest.
Arguments:
- features: bfloat16 [2, 32, 128, 64, 128], P('role', None, 'dev'), may hold values from -6 to 6
- labels: bfloat16 [2, 128, 64, 128], P('role', 'dev'), may hold values from 0 to 1
- crop_block: int32 [2, 64, 64], P('role'), may hold values from -1 to 15, as said below
- weight: float32 [64, 864], P('dev'), may hold values from -0.21875 to 0.21875
- gain: float32 [64], P('dev'), may hold values from 0.1 to 1.9
- shift: float32 [64], P('dev'), may hold values from -3 to 3
- head: float32 [64], P('dev'), may hold values from -1.5 to 1.5
- run_mean: float32 [64], P('dev'), may hold values from -2 to 2
- run_var: float32 [64], P('dev'), may hold values from 0.5 to 2
Outputs:
- scores: float32 [2, 128, 64, 128], P('role', 'dev')
- weight_grad: float32 [64, 864], P('dev')
- vector_grad: float32 [64, 3], P('dev')
The draws below stay inside these ranges and needn't reach their ends.
Inputs may be any that keep to these rules, and one draw needn't show every extreme that they name: crop_block[g, s, t] >= 0 is the row block b that source s of group g sends to learner t; -1 means no crop. Source s always sends to learner s, and to between 16 and 48 learners in all.
All inputs are finite; a program needn't handle non-finite values.
Results may differ from the reference program's by a relative error of at most 0.002.
The reference program's roundings to bfloat16 on the way count: a program that leaves them out, or rounds other values in their place, can miss the bound.
Values may be sent and summed in bfloat16 or wider, within the bound.
No kernel may reach another device: no remote copies, remote signals or barrier semaphores. Data moves between devices by JAX's collectives and lax.ppermute only.
A program may use at most 128 MiB of HBM per device.

```python
import math
import jax
import jax.numpy as jnp
from jax import lax

CI = 32
CO = 64
ZD = 2
YS = 64
XS = 128
CY = 4
Z = 128
N_ROLE = 2
N_DEV = 64


def draw_crop_block(key, part):
    subkeys = jax.random.split(jax.random.fold_in(key, 17), 3)
    counts = jax.random.randint(subkeys[0], (N_ROLE, N_DEV, 1), N_DEV // 4, 3 * N_DEV // 4 + 1)
    offsets = jnp.arange(N_DEV)
    scores = jax.random.randint(subkeys[1], (N_ROLE, N_DEV, N_DEV), 0, 1 << 20) * N_DEV + offsets
    scores = jnp.where(offsets == 0, -1, scores)
    ranking = jnp.sum((scores[..., None, :] < scores[..., :, None]).astype(jnp.int32), axis=-1)
    chosen = ranking < counts
    distance = (offsets[None, :] - offsets[:, None]) % N_DEV
    distance = jnp.broadcast_to(distance, (N_ROLE, N_DEV, N_DEV)).astype(jnp.int32)
    picked = jnp.take_along_axis(chosen, distance, axis=2)
    blocks = jax.random.randint(subkeys[2], (N_ROLE, N_DEV, N_DEV), 0, YS // CY)
    return jnp.where(picked, blocks, -1).astype(jnp.int32)


def block_scale(stream_key, shape, cuts, least, largest):
    def one(dim, blocks):
        draws = jax.random.uniform(jax.random.fold_in(jax.random.fold_in(stream_key, 6), dim), (blocks,), jnp.float32, least / len(cuts), largest / len(cuts))
        return jnp.repeat(jnp.exp(draws), shape[dim] // blocks).reshape((-1,) + (1,) * (len(shape) - dim - 1))

    factor_of = one(*cuts[0])
    for cut in cuts[1:]:
        factor_of = factor_of * one(*cut)
    return factor_of


def bell_draw(stream_key, shape, spread, reach, shards=(), kind=jnp.bfloat16):
    entries = jax.random.normal(stream_key, shape, jnp.float32) * spread
    if len(shards) > 0:
        entries = block_scale(stream_key, shape, shards, -0.22, 0.18) * entries
    return jnp.clip(entries, min=-reach, max=reach).astype(kind)


def setup_inputs(seed: int = 0) -> dict:
    splits = jax.random.split(jax.random.key(seed), 10)
    features = bell_draw(splits[0], (N_ROLE, CI, Z, YS, XS), 1.0, 6.0, ((0, 2), (2, 64)))
    labels = jnp.clip(1.0 * jax.random.uniform(splits[1], (N_ROLE, Z, YS, XS), jnp.float32) ** block_scale(splits[1], (N_ROLE, Z, YS, XS), ((0, 2), (1, 64)), -0.2, 0.2), 0.0, 1.0).astype(jnp.bfloat16)
    crop_block = draw_crop_block(jax.random.fold_in(splits[9], 71), 0)
    weight = bell_draw(splits[3], (CO, 27 * CI), (27 * CI) ** -0.5, 0.21875, ((0, 64),), jnp.float32)
    gain = jnp.clip(1.0 + 0.18 * jax.random.normal(splits[4], (CO,), jnp.float32), 0.1, 1.9)
    shift = bell_draw(splits[5], (CO,), 0.5, 3.0, ((0, 64),), jnp.float32)
    head = bell_draw(splits[6], (CO,), 0.25, 1.5, ((0, 64),), jnp.float32)
    run_mean = bell_draw(splits[7], (CO,), 0.3, 2.0, ((0, 64),), jnp.float32)
    run_var = jnp.clip(jnp.exp(math.log(2.0) - 1.3862944 * jax.random.uniform(splits[8], (CO,), jnp.float32) ** block_scale(splits[8], (CO,), ((0, 64),), -0.2, 0.2)), 0.5, 2.0)
    return {"features": features, "labels": labels, "crop_block": crop_block, "weight": weight, "gain": gain, "shift": shift, "head": head, "run_mean": run_mean, "run_var": run_var}


epsilon = 1e-05

def conv_field(field, weight_matrix):
    filter_weight = weight_matrix.astype(jnp.float32).reshape(CO, 3, 3, 3, CI).transpose(0, 4, 1, 2, 3)
    return lax.conv_general_dilated(field.astype(jnp.float32), filter_weight, (1, 1, 1), ((1, 1), (1, 1), (1, 1)), dimension_numbers=('NCDHW', 'OIDHW', 'NCDHW'), precision=lax.Precision.HIGHEST)

def reference(features, labels, crop_block, weight, gain, shift, head, run_mean, run_var):
    weight_f = lax.optimization_barrier(weight.astype(jnp.bfloat16)).astype(jnp.float32)
    stacked = jnp.stack([gain, shift, head, run_mean, run_var]).astype(jnp.bfloat16)
    vector_f = lax.optimization_barrier(stacked).astype(jnp.float32)
    gain_value = vector_f[0]
    shift_value = vector_f[1]
    head_value = vector_f[2]
    mean_value = vector_f[3]
    spread_value = vector_f[4]
    block_count = YS // CY
    crop_cells = ZD * CY * XS
    sources = jnp.arange(N_DEV)
    score_list = []
    weight_total = jnp.zeros((CO, 27 * CI), jnp.float32)
    vector_total = jnp.zeros((CO, 3), jnp.float32)
    for group_index in range(N_ROLE):
        grouped_feature_field = features[group_index]
        conv_whole = conv_field(grouped_feature_field[None], weight_f)[0]
        normed = (conv_whole - mean_value[:, None, None, None]) * lax.rsqrt(spread_value + epsilon)[:, None, None, None]
        hidden = jax.nn.relu(gain_value[:, None, None, None] * normed + shift_value[:, None, None, None])
        score_list.append(jnp.einsum('c,czyx->zyx', head_value, hidden, precision=lax.Precision.HIGHEST))
        pieces = grouped_feature_field.reshape(CI, N_DEV, ZD, block_count, CY, XS).transpose(1, 3, 0, 2, 4, 5)
        pieces = pieces.reshape(N_DEV * block_count, CI, ZD, CY, XS)
        crop_out = conv_field(pieces, weight_f).astype(jnp.bfloat16).reshape(N_DEV, block_count, CO, ZD, CY, XS)
        label_blocks = labels[group_index].reshape(N_DEV, ZD, block_count, CY, XS).transpose(0, 2, 1, 3, 4)

        def learner(running, column):
            live_flags = column >= 0
            chosen = jnp.maximum(column, 0).astype(jnp.int32)
            ufield = crop_out[sources, chosen].astype(jnp.float32)
            target = label_blocks[sources, chosen].astype(jnp.float32)
            live_weights = live_flags.astype(jnp.float32)
            cell_count = jnp.sum(live_weights) * crop_cells
            mask = live_weights[:, None, None, None, None]

            def loss_fn(field_in, gain_in, shift_in, head_input_channels):
                channel_mean = lax.optimization_barrier(jnp.sum(field_in * mask, axis=(0, 2, 3, 4))) / cell_count
                centred = field_in - channel_mean[None, :, None, None, None]
                channel_var = lax.optimization_barrier(jnp.sum((centred * mask) ** 2, axis=(0, 2, 3, 4))) / cell_count
                normal = centred * lax.rsqrt(channel_var + epsilon)[None, :, None, None, None]
                hidden_width = jax.nn.relu(gain_in[None, :, None, None, None] * normal + shift_in[None, :, None, None, None])
                ranked_crops = jnp.einsum('bjnkw,j->bnkw', hidden_width, head_input_channels, precision=lax.Precision.HIGHEST)
                return 0.5 * jnp.sum(live_weights[:, None, None, None] * (ranked_crops - target) ** 2) / cell_count
            loss_value, pull = jax.vjp(loss_fn, ufield, gain_value, shift_value, head_value)
            dfield, dgain, dshift, dhead = pull(jnp.ones_like(loss_value))
            dfield = lax.optimization_barrier(dfield.astype(jnp.bfloat16)).astype(jnp.float32)
            grads_sum, vector_sum = running
            grads_sum = grads_sum.at[sources, chosen].add(dfield * mask)
            vector_sum = vector_sum + jnp.stack([dgain, dshift, dhead], 1)
            return ((grads_sum, vector_sum), None)
        initial = (jnp.zeros((N_DEV, block_count, CO, ZD, CY, XS), jnp.float32), jnp.zeros((CO, 3), jnp.float32))
        (grads_sum, vector_sum), _ = lax.scan(learner, initial, crop_block[group_index].T)
        _, pull_weight = jax.vjp(lambda kernel_matrix: conv_field(pieces, kernel_matrix), weight_f)
        weight_part, = pull_weight(grads_sum.reshape(N_DEV * block_count, CO, ZD, CY, XS))
        weight_total = weight_total + weight_part
        vector_total = vector_total + vector_sum
    return (jnp.stack(score_list), weight_total, vector_total)
```

```python
import jax
import jax.numpy as jnp
from jax import lax
from jax.experimental import pallas as pl
from jax.experimental.pallas import tpu as pltpu
from jax.sharding import PartitionSpec as P


CY = 4
EPS = 1e-05
SENT = 48
F32 = jnp.float32
BF16 = jnp.bfloat16
PARAMS = pltpu.VMEM((512, 128), F32)
ANY = pl.BlockSpec(memory_space=pl.ANY)
VMEM = pl.BlockSpec(memory_space=pltpu.VMEM)
SMEM = pl.BlockSpec(memory_space=pltpu.SMEM)


def lane_iota(rows=64):
    return lax.broadcasted_iota(jnp.int32, (rows, 128), 1)


def roll_lanes(x, shift):
    shift %= 128
    return x if shift == 0 else pltpu.roll(x, shift, 1)


def load_params(w_ref, p_ref):
    wide = w_ref[...].astype(F32)
    p_ref[...] = wide.reshape(wide.shape[0] * 8, 128)


def chunk(p_ref, k):
    return p_ref[pl.ds(k, 64, stride=8), :]


def column(p_ref, k):
    return chunk(p_ref, 6)[:, 96 + k : 97 + k]


def fill_taps(p_ref, taps_ref):
    block = lane_iota() // 32
    chunks = [chunk(p_ref, k) for k in range(7)]
    for a in range(3):
        for c in range(3):
            out = jnp.zeros((64, 128), F32)
            for b in range(3):
                tap = 9 * a + 3 * b + c
                moved = roll_lanes(chunks[tap // 4], 32 * (b - tap % 4))
                out = jnp.where(block == b, moved, out)
            taps_ref[c, a] = out


def banded(taps_ref, c, a, yo):
    block = lane_iota() // 32
    v = roll_lanes(taps_ref[c, a], 32 * (yo - 1))
    if yo == 0:
        v = jnp.where(block == 3, 0.0, v)
    if yo == 3:
        v = jnp.where(block == 0, 0.0, v)
    return v


def pack_kernel(weight_ref, gain_ref, shift_ref, head_ref, mean_ref, var_ref, out_ref):
    lane = lax.broadcasted_iota(jnp.int32, (8, 128), 1)
    sub = lax.broadcasted_iota(jnp.int32, (8, 128), 0)
    out = jnp.zeros((8, 128), F32)
    for k in range(6):
        out = jnp.where(sub == k, weight_ref[:, 128 * k : 128 * k + 128], out)
    tail = jnp.concatenate([weight_ref[:, 768:864], jnp.zeros((1, 32), F32)], axis=1)
    out = jnp.where(sub == 6, tail, out)
    for k, ref in enumerate((gain_ref, shift_ref, head_ref, mean_ref, var_ref)):
        out = jnp.where((sub == 6) & (lane == 96 + k), ref[...].reshape(1, 1), out)
    out_ref[...] = jnp.broadcast_to(out.astype(BF16)[None], out_ref.shape)


def shifted(v):
    lane = lax.broadcasted_iota(jnp.int32, v.shape, 1)
    left = jnp.where(lane == 0, 0.0, pltpu.roll(v, 1, 1))
    right = jnp.where(lane == 127, 0.0, pltpu.roll(v, 127, 1))
    return left, v, right


def prep_kernel(slab_ref, x_ref, wide_ref):
    channels, _, height, _ = slab_ref.shape
    wide_ref[...] = slab_ref[:, 0].astype(F32).reshape(channels * height, 128)
    for y in range(height):
        v = wide_ref[pl.ds(y, channels, stride=height), :]
        rows = slice(32 * (y % CY), 32 * (y % CY) + 32)
        lanes = slice(128 * (y // CY), 128 * (y // CY) + 128)
        for c, w in enumerate(shifted(v)):
            x_ref[c, 0, rows, lanes] = w.astype(BF16)


def crop_conv_kernel(w_ref, x_ref, u_ref, stats_ref, p_ref, taps_ref, t_ref, s1_ref, m2_ref):
    load_params(w_ref, p_ref)
    fill_taps(p_ref, taps_ref)
    for zo in range(2):
        for yo in range(4):
            row = 64 * (4 * zo + yo)
            for c in range(3):
                for z in range(2):
                    col = 256 * c + 128 * z
                    v = banded(taps_ref, c, z - zo + 1, yo)
                    t_ref[row : row + 64, col : col + 128] = v.astype(BF16)
    s1_ref[...] = jnp.zeros((64, 128), F32)
    m2_ref[...] = jnp.zeros((64, 128), F32)
    lanes = lane_iota()

    def convolve(p):
        dst = pl.multiple_of(256 * p, 128)
        x = jnp.concatenate(
            [x_ref[c, z, :, pl.ds(dst, 256)] for c in range(3) for z in range(2)], axis=0
        )
        u = jnp.dot(t_ref[...], x, preferred_element_type=F32).astype(BF16)
        for half in range(2):
            for j in range(8):
                u_ref[pl.ds(pl.multiple_of(64 * (2 * p + half), 64), 64), 128 * j : 128 * j + 128] = u[
                    64 * j : 64 * j + 64, 128 * half : 128 * half + 128
                ]

    def statistics(p, u):
        for half in range(2):
            parts = [
                u[64 * half : 64 * half + 64, 128 * j : 128 * j + 128].astype(F32)
                for j in range(8)
            ]
            total = jnp.sum(sum(parts), axis=1, keepdims=True)
            mean = total * (1.0 / 1024)
            square = jnp.zeros((64, 128), F32)
            for part in parts:
                d = part - mean
                square = square + d * d
            here = lanes == 2 * p + half
            s1_ref[...] = jnp.where(here, total, s1_ref[...])
            m2_ref[...] = jnp.where(here, jnp.sum(square, axis=1, keepdims=True), m2_ref[...])

    convolve(0)

    def step(p, _):
        before = u_ref[pl.ds(pl.multiple_of(128 * p, 128), 128), :]
        convolve(p + 1)
        statistics(p, before)
        return 0

    pairs = u_ref.shape[0] // 128
    lax.fori_loop(0, pairs - 1, step, 0)
    statistics(pairs - 1, u_ref[128 * (pairs - 1) :, :])
    stats = jnp.concatenate([s1_ref[...], m2_ref[...]], axis=0).T[:16]

    def spread(s, _):
        stats_ref[s] = stats
        return 0

    lax.fori_loop(0, stats_ref.shape[0], spread, 0, unroll=8)


def score_kernel(
    w_ref, x_ref, below_ref, above_ref, cbt_ref, _, out_ref, hot_ref, p_ref, taps_ref, t_ref, f_ref
):
    learners, sources = cbt_ref.shape
    entries = hot_ref.shape[1]
    live = jnp.where(cbt_ref[...] >= 0, 1.0, 0.0)
    earlier = lax.broadcasted_iota(jnp.int32, (learners, learners), 1) < lax.broadcasted_iota(
        jnp.int32, (learners, learners), 0
    )
    place = jnp.dot(
        jnp.where(earlier, 1.0, 0.0).astype(BF16), live.astype(BF16), preferred_element_type=F32
    )
    place = jnp.where(live > 0, place, -1.0).astype(BF16)
    lane = lax.broadcasted_iota(jnp.int32, (sources, entries), 1)
    start = SENT * lax.broadcasted_iota(jnp.int32, (sources, entries), 0)
    expand = jnp.where((lane >= start) & (lane < start + SENT), 1.0, 0.0).astype(BF16)
    wanted = jnp.dot(place, expand, preferred_element_type=F32)
    slot = (lax.broadcasted_iota(jnp.int32, (8, entries), 1) % SENT).astype(F32)[0:1]
    hot_ref[...] = jnp.where(wanted == slot, 1.0, 0.0).astype(BF16)
    load_params(w_ref, p_ref)
    fill_taps(p_ref, taps_ref)
    block = lane_iota() // 32
    zero = jnp.zeros((64, 128), F32)
    for zo in range(2):
        for yo in range(4):
            row = slice(64 * (4 * zo + yo), 64 * (4 * zo + yo) + 64)
            for c in range(3):
                edges = []
                for zz in range(4):
                    a = zz - zo
                    inside = 0 <= a <= 2
                    v = banded(taps_ref, c, a, yo) if inside else zero
                    col = 128 * (4 * c + zz)
                    t_ref[row, col : col + 128] = v.astype(BF16)
                    odd = zz % 2
                    if inside and yo == 0:
                        v = roll_lanes(taps_ref[c, a], 64 * odd)
                        edges.append(jnp.where(block == 2 * odd, v, 0.0))
                    elif inside and yo == 3:
                        v = roll_lanes(taps_ref[c, a], 64 * odd - 32)
                        edges.append(jnp.where(block == 2 * odd + 1, v, 0.0))
                    else:
                        edges.append(zero)
                for k in range(2):
                    col = 1536 + 128 * (2 * c + k)
                    v = edges[2 * k] + edges[2 * k + 1]
                    t_ref[row, col : col + 128] = v.astype(BF16)
    gain, shift, head, mean, var = (column(p_ref, k) for k in range(5))
    alpha = gain * lax.rsqrt(var + EPS)
    beta = shift - mean * alpha
    alpha = jnp.broadcast_to(alpha, (64, 128))
    beta = jnp.broadcast_to(beta, (64, 128))
    head = jnp.broadcast_to(head, (64, 128))

    count = x_ref.shape[3] // 128
    empty = jnp.zeros((128, 128), BF16)
    for c in range(3):
        for zz in range(4):
            f_ref[c, zz, :, 0:128] = empty
            f_ref[c, zz, :, 128 * (count + 1) : 128 * (count + 2)] = empty
        for z in range(2):
            f_ref[c, 1 + z, :, 128 : 128 * (count + 1)] = x_ref[c, z]

    def halo(b, _):
        src = pl.multiple_of(128 * b, 128)
        dst = pl.multiple_of(128 * b + 128, 128)
        for zz, ref in ((0, below_ref), (3, above_ref)):
            v = ref[0, :, pl.ds(src, 128)].astype(F32)
            for c, w in enumerate(shifted(v)):
                f_ref[c, zz, :, pl.ds(dst, 128)] = w.astype(BF16)
        return 0

    lax.fori_loop(0, count, halo, 0)

    def step(p, _):
        at = pl.multiple_of(256 * p, 128)
        pairs = [(c, zz) for c in range(3) for zz in range(4)]
        rows = [f_ref[c, zz, :, pl.ds(at + 128, 256)] for c, zz in pairs]
        for c, zz in pairs:
            rows.append(f_ref[c, zz, 96:128, pl.ds(at, 256)])
            rows.append(f_ref[c, zz, 0:32, pl.ds(at + 256, 256)])
        out = jnp.dot(t_ref[...], jnp.concatenate(rows, axis=0), preferred_element_type=F32)
        for half in range(2):
            for j in range(8):
                v = out[64 * j : 64 * j + 64, 128 * half : 128 * half + 128]
                h = jnp.maximum(v * alpha + beta, 0.0) * head
                out_ref[j // 4, 2 * p + half, j % 4 : j % 4 + 1, :] = jnp.sum(
                    h, axis=0, keepdims=True
                )
        return 0

    lax.fori_loop(0, count // 2, step, 0)


def exact_dot(a, v):
    hi = v.astype(BF16)
    rest = v - hi.astype(F32)
    mid = rest.astype(BF16)
    low = (rest - mid.astype(F32)).astype(BF16)
    out = jnp.dot(a, low, preferred_element_type=F32)
    out = out + jnp.dot(a, mid, preferred_element_type=F32)
    return out + jnp.dot(a, hi, preferred_element_type=F32)


def learner_kernel(
    cb_ref, w_ref, r_ref, cbt_ref, u_ref, lab_ref,
    send_ref, g_ref, mr_ref, vec_ref, inv_ref, row_ref,
    p_ref, acc_ref, part_ref, coef_ref, scale_ref, al_ref, be_ref, hd_ref, r0_ref, ru_ref,
):
    load_params(w_ref, p_ref)
    lanes = lane_iota()
    learners, sources = cbt_ref.shape
    entries = r_ref.shape[0]
    lane = lax.broadcasted_iota(jnp.int32, (sources, entries), 1)
    source = lax.broadcasted_iota(jnp.int32, (sources, entries), 0)
    expand = jnp.where(lane // 16 == source, 1.0, 0.0).astype(BF16)
    wanted = jnp.dot(cbt_ref[...].astype(BF16), expand, preferred_element_type=F32)
    which = lax.broadcasted_iota(jnp.int32, (learners, entries), 1) % 16
    onehot = jnp.where(wanted == which.astype(F32), 1.0, 0.0).astype(BF16)
    number = jnp.sum(jnp.where(cbt_ref[...] >= 0, 1.0, 0.0), axis=1, keepdims=True)
    r = r_ref[...]
    means = r * (1.0 / 1024)
    centre = jnp.mean(means, axis=0, keepdims=True)
    d = means - centre
    rolled = pltpu.roll(d, 64, 1)
    low_half = lax.broadcasted_iota(jnp.int32, (entries, 128), 1) < 64
    v = jnp.where(low_half, d, means + rolled * rolled)
    p = exact_dot(onehot, v) / number
    first = jnp.where(lanes < 64, p, 0.0)
    mu = first + centre
    var = pltpu.roll(p, 64, 1) - first * first
    rstd = lax.rsqrt(jnp.maximum(var, 0.0) + EPS)
    both = jnp.where(lanes < 64, mu, pltpu.roll(rstd, 64, 1))
    both_t = jnp.concatenate([both, jnp.zeros((128 - learners, 128), F32)], axis=0).T
    mr_ref[...] = both_t
    inverse = jnp.broadcast_to(1.0 / (number * 1024.0), (learners, 128))
    inverse = jnp.concatenate([inverse, jnp.zeros((128 - learners, 128), F32)], axis=0).T
    inv_ref[...] = inverse[:8]
    row_ref[...] = jnp.full((8, 128), -1, jnp.int32)
    gain, shift, head = (jnp.broadcast_to(column(p_ref, k), (64, 128)) for k in range(3))
    alpha = gain * both_t[64:]
    al_ref[...] = alpha
    be_ref[...] = shift - alpha * both_t[:64]
    hd_ref[...] = head
    r0_ref[...] = jnp.zeros((64, 128), F32)
    ru_ref[...] = jnp.zeros((64, 128), F32)
    acc_ref[...] = jnp.zeros_like(acc_ref)
    part_ref[...] = jnp.zeros_like(part_ref)
    live = cb_ref[2 * learners]

    def reduce(k, e):
        here = lanes == k
        r0 = jnp.sum(part_ref[2 * e], axis=1, keepdims=True)
        rh = jnp.sum(part_ref[2 * e + 1], axis=1, keepdims=True)
        r0_ref[...] = jnp.where(here, r0, r0_ref[...])
        ru_ref[...] = jnp.where(here, rh, ru_ref[...])

    def fetch(k):
        t = cb_ref[jnp.minimum(k, live - 1)]
        index = jnp.full((64, 128), t, jnp.int32)
        inv = jnp.take_along_axis(inv_ref[...], index[:8], axis=1)
        al = jnp.take_along_axis(al_ref[...], index, axis=1)
        be = jnp.take_along_axis(be_ref[...], index, axis=1)
        return jnp.where(k < live, inv, 0.0), al, be, hd_ref[...] * al

    def keep(e, coefficients):
        scale_ref[e] = coefficients[0]
        for n in range(3):
            coef_ref[3 * e + n] = coefficients[1 + n]

    def learner(k, e):
        t = cb_ref[jnp.minimum(k, live - 1)]
        b = cb_ref[learners + t]
        at = pl.multiple_of(b * 128, 128)
        row = pl.multiple_of(b * 64, 64)
        row_ref[...] = jnp.where(lanes[:8] == t, b, row_ref[...])
        al, be, c1 = (coef_ref[3 * e + n] for n in range(3))
        inv = scale_ref[e, 0:1]
        hd = hd_ref[...]
        r0 = jnp.zeros((64, 128), F32)
        rh = jnp.zeros((64, 128), F32)
        for j in range(8):
            us = u_ref[pl.ds(row, 64), 128 * j : 128 * j + 128].astype(F32)
            h = jnp.maximum(us * al + be, 0.0)
            score = jnp.sum(h * hd, axis=0, keepdims=True)
            res = (score - lab_ref[b, j : j + 1, :]) * inv
            m = jnp.where(h > 0, res, 0.0)
            r0 = r0 + m
            rh = rh + h * res
            acc_ref[64 * j : 64 * j + 64, pl.ds(at, 128)] += c1 * m
        part_ref[2 * e] = r0
        part_ref[2 * e + 1] = rh

    def step(i, _):
        for e in range(2):
            reduce(2 * i - 2 + e, e)
        following = [fetch(2 * i + 2 + e) for e in range(2)]
        for e in range(2):
            learner(2 * i + e, e)
            keep(e, following[e])
        return 0

    for e in range(2):
        keep(e, fetch(e))
    steps = (live + 1) // 2
    lax.fori_loop(0, steps, step, 0)
    for e in range(2):
        reduce(2 * steps - 2 + e, e)
    r0 = r0_ref[...]
    r1 = (ru_ref[...] - shift * r0) / gain
    sends = send_ref.shape[1]
    out = jnp.concatenate([r0, r1], axis=0).T[:sends].astype(BF16)

    def spread(s, _):
        send_ref[s] = out
        return 0

    lax.fori_loop(0, send_ref.shape[0], spread, 0, unroll=8)
    dgain = jnp.sum(head * r1, axis=1, keepdims=True)
    dshift = jnp.sum(head * r0, axis=1, keepdims=True)
    dhead = jnp.sum(gain * r1 + shift * r0, axis=1, keepdims=True)
    vec_ref[...] = jnp.where(
        lanes == 96, dgain, jnp.where(lanes == 97, dshift, jnp.where(lanes == 98, dhead, 0.0))
    )
    g_ref[...] = acc_ref[...].astype(BF16)


def gradient_kernel(
    w_ref, r_ref, hot_ref, mr_ref, inv_ref, cb_ref, g_ref, u_ref, x_ref, vec_ref,
    out_ref, p_ref, full_ref, dt_ref, row_ref,
):
    load_params(w_ref, p_ref)
    learners = hot_ref.shape[0]
    total = jnp.dot(hot_ref[...], r_ref[...], preferred_element_type=F32)
    total = jnp.concatenate([total, jnp.zeros((128 - learners, 128), F32)], axis=0).T
    gain, head = (jnp.broadcast_to(column(p_ref, k), (64, 128)) for k in (0, 2))
    factor = gain * head * inv_ref[0:1, :]
    first = factor * total[:64]
    second = factor * total[64:]
    mu = mr_ref[:64]
    rstd = mr_ref[64:]
    slope = rstd * rstd * second
    offset = rstd * first - slope * mu
    row = cb_ref[0:1, :]

    def block(b, _):
        at = pl.multiple_of(b * 128, 128)
        row64 = pl.multiple_of(b * 64, 64)
        here = row == b
        e = jnp.broadcast_to(jnp.sum(jnp.where(here, offset, 0.0), axis=1, keepdims=True), (64, 128))
        f = jnp.broadcast_to(jnp.sum(jnp.where(here, slope, 0.0), axis=1, keepdims=True), (64, 128))
        for j in range(8):
            rows = slice(64 * j, 64 * j + 64)
            v = g_ref[rows, pl.ds(at, 128)].astype(F32) - e
            v = v - f * u_ref[pl.ds(row64, 64), 128 * j : 128 * j + 128].astype(F32)
            full_ref[rows, pl.ds(at, 128)] = v.astype(BF16)
        return 0

    lax.fori_loop(0, 16, block, 0)
    for c in range(3):
        dt_ref[:, 256 * c : 256 * c + 256] = lax.dot_general(
            full_ref[...],
            jnp.concatenate([x_ref[c, 0], x_ref[c, 1]], axis=0),
            (((1,), (1,)), ((), ())),
            preferred_element_type=F32,
        )
    blocks = lane_iota() // 32
    outs = [jnp.zeros((64, 128), F32) for _ in range(6)] + [vec_ref[...]]
    for c in range(3):
        for a in range(3):
            acc = jnp.zeros((64, 128), F32)
            for zo in range(2):
                z = zo + a - 1
                if not 0 <= z <= 1:
                    continue
                for yo in range(4):
                    j = 4 * zo + yo
                    col = 256 * c + 128 * z
                    v = roll_lanes(dt_ref[64 * j : 64 * j + 64, col : col + 128], -32 * (yo - 1))
                    if yo == 0:
                        v = jnp.where(blocks == 0, 0.0, v)
                    if yo == 3:
                        v = jnp.where(blocks == 2, 0.0, v)
                    acc = acc + v
            for b in range(3):
                tap = 9 * a + 3 * b + c
                k = tap // 4
                outs[k] = jnp.where(
                    blocks == tap % 4, roll_lanes(acc, 32 * (tap % 4 - b)), outs[k]
                )
    outs.append(jnp.zeros((64, 128), F32))
    for k in range(8):
        row_ref[pl.ds(k, 64, stride=8), :] = outs[k]
    packed = row_ref[...].astype(BF16)
    for role in range(out_ref.shape[0] // 512):
        out_ref[512 * role : 512 * role + 512, :] = packed


def finish_kernel(r_ref, weight_ref, vector_ref):
    total = jnp.sum(r_ref[...].astype(F32), axis=0)
    for k in range(6):
        weight_ref[:, 128 * k : 128 * k + 128] = total[k : k + 1]
    weight_ref[:, 768:864] = total[6:7, :96]
    vector_ref[...] = total[6:7, 96:99]


def per_device(features, labels, crop_block, weight, gain, shift, head, run_mean, run_var):
    devices = lax.axis_size("dev")
    roles = lax.axis_size("role")
    rows = pl.pallas_call(
        pack_kernel,
        out_shape=jax.ShapeDtypeStruct((devices, 8, 128), BF16),
        in_specs=[VMEM] * 6,
        out_specs=VMEM,
        name="pack",
    )(weight, gain, shift, head, run_mean, run_var)
    params = lax.all_to_all(rows, "dev", 0, 0, tiled=True)

    slab = features[0]
    channels, planes, height, columns = slab.shape
    count = height // CY
    cells = count * columns
    field = pl.pallas_call(
        prep_kernel,
        out_shape=jax.ShapeDtypeStruct((3, planes, CY * channels, cells), BF16),
        grid=(planes,),
        in_specs=[pl.BlockSpec((channels, 1, height, columns), lambda z: (0, z, 0, 0))],
        out_specs=pl.BlockSpec((3, 1, CY * channels, cells), lambda z: (0, z, 0, 0)),
        scratch_shapes=[pltpu.VMEM((channels * height, columns), F32)],
        cost_estimate=pl.CostEstimate(flops=10**7, bytes_accessed=4 << 20, transcendentals=0),
        name="prep",
    )(slab)

    table = crop_block[0]
    own_index = lax.axis_index("dev")
    mine = lax.dynamic_slice_in_dim(table, own_index, 1, 0)[0]
    live = mine >= 0
    places = jnp.arange(devices)
    before = jnp.sum(live[None, :] & (places[None, :] < places[:, None]), axis=1)
    at = live[None, :] & (before[None, :] == places[:, None])
    order = jnp.sum(jnp.where(at, places[None, :], 0), axis=1)
    lists = jnp.concatenate([order, mine, jnp.sum(live.astype(jnp.int32))[None]]).astype(jnp.int32)
    turned = table.T.astype(F32)
    targets = labels[0].reshape(planes, count, CY, columns).transpose(1, 0, 2, 3)
    targets = targets.reshape(count, planes * CY, columns).astype(F32)

    u, stats = pl.pallas_call(
        crop_conv_kernel,
        out_shape=(
            jax.ShapeDtypeStruct((64 * count, 1024), BF16),
            jax.ShapeDtypeStruct((devices, count, 128), F32),
        ),
        in_specs=[VMEM] * 2,
        out_specs=(VMEM, VMEM),
        scratch_shapes=[
            PARAMS,
            pltpu.VMEM((3, 3, 64, 128), F32),
            pltpu.VMEM((512, 768), BF16),
            pltpu.VMEM((64, 128), F32),
            pltpu.VMEM((64, 128), F32),
        ],
        cost_estimate=pl.CostEstimate(flops=2 * 512 * 768 * cells, bytes_accessed=8 << 20, transcendentals=0),
        name="crop_conv",
    )(params, field)

    gathered = lax.all_to_all(stats, "dev", 0, 0, tiled=True)
    gathered = gathered.reshape(devices * count, 128)
    plane = field[1]
    below = lax.ppermute(plane[-1:], "dev", [(i, i + 1) for i in range(devices - 1)])
    above = lax.ppermute(plane[:1], "dev", [(i + 1, i) for i in range(devices - 1)])

    send, g, mr, vec, inverse, mine_row = pl.pallas_call(
        learner_kernel,
        out_shape=(
            jax.ShapeDtypeStruct((devices, SENT, 128), BF16),
            jax.ShapeDtypeStruct((512, cells), BF16),
            jax.ShapeDtypeStruct((128, 128), F32),
            jax.ShapeDtypeStruct((64, 128), F32),
            jax.ShapeDtypeStruct((8, 128), F32),
            jax.ShapeDtypeStruct((8, 128), jnp.int32),
        ),
        in_specs=[SMEM] + [VMEM] * 5,
        out_specs=(VMEM,) * 6,
        scratch_shapes=[
            PARAMS,
            pltpu.VMEM((512, cells), F32),
            pltpu.VMEM((4, 64, 128), F32),
            pltpu.VMEM((6, 64, 128), F32),
            pltpu.VMEM((2, 8, 128), F32),
        ]
        + [pltpu.VMEM((64, 128), F32)] * 5,
        cost_estimate=pl.CostEstimate(flops=10**10, bytes_accessed=8 << 20, transcendentals=0),
        name="learner",
    )(lists, params, gathered, turned, u, targets)

    arrived = lax.all_to_all(send, "dev", 0, 0, tiled=True)

    scores, hot = pl.pallas_call(
        score_kernel,
        out_shape=(
            jax.ShapeDtypeStruct((planes, count, CY, columns), F32),
            jax.ShapeDtypeStruct((devices, devices * SENT), BF16),
        ),
        in_specs=[VMEM] * 5 + [ANY],
        out_specs=(VMEM, VMEM),
        scratch_shapes=[
            PARAMS,
            pltpu.VMEM((3, 3, 64, 128), F32),
            pltpu.VMEM((512, 2304), BF16),
            pltpu.VMEM((3, planes + 2, CY * channels, cells + 256), BF16),
        ],
        cost_estimate=pl.CostEstimate(flops=2 * 512 * 2304 * cells, bytes_accessed=8 << 20, transcendentals=0),
        name="score",
    )(params, field, below, above, turned, vec)

    final = pl.pallas_call(
        gradient_kernel,
        out_shape=jax.ShapeDtypeStruct((roles * devices * 8, 128), BF16),
        in_specs=[VMEM] * 10,
        out_specs=VMEM,
        scratch_shapes=[
            PARAMS,
            pltpu.VMEM((512, cells), BF16),
            pltpu.VMEM((512, 768), F32),
            pltpu.VMEM((512, 128), F32),
        ],
        cost_estimate=pl.CostEstimate(flops=2 * 512 * 768 * cells, bytes_accessed=8 << 20, transcendentals=0),
        name="gradient",
    )(
        params,
        arrived.reshape(devices * SENT, 128),
        hot, mr, inverse, mine_row, g, u, field, vec,
    )
    final = lax.all_to_all(
        final.reshape(roles * devices, 8, 128), ("role", "dev"), 0, 0, tiled=True
    )
    weight_grad, vector_grad = pl.pallas_call(
        finish_kernel,
        out_shape=(
            jax.ShapeDtypeStruct((1, 864), F32),
            jax.ShapeDtypeStruct((1, 3), F32),
        ),
        in_specs=[VMEM],
        out_specs=(VMEM, VMEM),
        name="finish",
    )(final)
    return (scores.reshape(1, planes, height, columns), weight_grad, vector_grad)


def solution(mesh):
    in_specs = (
        P("role", None, "dev", None, None),
        P("role", "dev", None, None),
        P("role", None, None),
        P("dev", None),
        P("dev"),
        P("dev"),
        P("dev"),
        P("dev"),
        P("dev"),
    )
    out_specs = (P("role", "dev", None, None), P("dev", None), P("dev", None))
    return jax.shard_map(
        per_device, mesh=mesh, in_specs=in_specs, out_specs=out_specs, check_vma=False
    )
```

```python
import jax
import jax.numpy as jnp
from jax import lax
from jax.experimental import pallas as pl
from jax.experimental.pallas import tpu as pltpu
from jax.sharding import PartitionSpec as P


CY = 4
EPS = 1e-05
SENT = 48
F32 = jnp.float32
BF16 = jnp.bfloat16
PARAMS = pltpu.VMEM((512, 128), F32)
ANY = pl.BlockSpec(memory_space=pl.ANY)
VMEM = pl.BlockSpec(memory_space=pltpu.VMEM)
SMALL = pltpu.CompilerParams(vmem_limit_bytes=20 << 20)
HBM = pl.BlockSpec(memory_space=pltpu.HBM)
DMA = pltpu.SemaphoreType.DMA
SMEM = pl.BlockSpec(memory_space=pltpu.SMEM)


def near(x):
    return pltpu.with_memory_space_constraint(x, pltpu.VMEM)


def far(x):
    return pltpu.with_memory_space_constraint(x, pltpu.HBM)


def lane_iota(rows=64):
    return lax.broadcasted_iota(jnp.int32, (rows, 128), 1)


def roll_lanes(x, shift):
    shift %= 128
    return x if shift == 0 else pltpu.roll(x, shift, 1)


def load_params(w_ref, p_ref):
    wide = w_ref[...].astype(F32)
    p_ref[...] = wide.reshape(wide.shape[0] * 8, 128)


def chunk(p_ref, k):
    return p_ref[pl.ds(k, 64, stride=8), :]


def column(p_ref, k):
    return chunk(p_ref, 6)[:, 96 + k : 97 + k]


def fill_taps(p_ref, taps_ref):
    block = lane_iota() // 32
    chunks = [chunk(p_ref, k) for k in range(7)]
    for a in range(3):
        for c in range(3):
            out = jnp.zeros((64, 128), F32)
            for b in range(3):
                tap = 9 * a + 3 * b + c
                moved = roll_lanes(chunks[tap // 4], 32 * (b - tap % 4))
                out = jnp.where(block == b, moved, out)
            taps_ref[c, a] = out


def banded(taps_ref, c, a, yo):
    block = lane_iota() // 32
    v = roll_lanes(taps_ref[c, a], 32 * (yo - 1))
    if yo == 0:
        v = jnp.where(block == 3, 0.0, v)
    if yo == 3:
        v = jnp.where(block == 0, 0.0, v)
    return v


def pack_kernel(row_ref, out_ref):
    sub = lax.broadcasted_iota(jnp.int32, (8, 128), 0)
    out = jnp.zeros((8, 128), F32)
    for k in range(7):
        out = jnp.where(sub == k, row_ref[:, 128 * k : 128 * k + 128], out)
    out_ref[...] = jnp.broadcast_to(out.astype(BF16)[None], out_ref.shape)


def shifted(v):
    lane = lax.broadcasted_iota(jnp.int32, v.shape, 1)
    left = jnp.where(lane == 0, 0.0, pltpu.roll(v, 1, 1))
    right = jnp.where(lane == 127, 0.0, pltpu.roll(v, 127, 1))
    return left, v, right


def prep_kernel(slab_ref, x_ref, wide_ref):
    channels, _, height, _ = slab_ref.shape
    wide_ref[...] = slab_ref[:, 0].astype(F32).reshape(channels * height, 128)
    for y in range(height):
        v = wide_ref[pl.ds(y, channels, stride=height), :]
        rows = slice(32 * (y % CY), 32 * (y % CY) + 32)
        lanes = slice(128 * (y // CY), 128 * (y // CY) + 128)
        for c, w in enumerate(shifted(v)):
            x_ref[c, 0, rows, lanes] = w.astype(BF16)


def crop_conv_kernel(
    w_ref, x_ref, out_ref, stats_ref, p_ref, taps_ref, t_ref, s1_ref, m2_ref, u_ref, sem
):
    load_params(w_ref, p_ref)
    fill_taps(p_ref, taps_ref)
    for zo in range(2):
        for yo in range(4):
            row = 64 * (4 * zo + yo)
            for c in range(3):
                for z in range(2):
                    col = 256 * c + 128 * z
                    v = banded(taps_ref, c, z - zo + 1, yo)
                    t_ref[row : row + 64, col : col + 128] = v.astype(BF16)
    s1_ref[...] = jnp.zeros((64, 128), F32)
    m2_ref[...] = jnp.zeros((64, 128), F32)
    lanes = lane_iota()

    def convolve(p):
        dst = pl.multiple_of(256 * p, 128)
        x = jnp.concatenate(
            [x_ref[c, z, :, pl.ds(dst, 256)] for c in range(3) for z in range(2)], axis=0
        )
        u = jnp.dot(t_ref[...], x, preferred_element_type=F32).astype(BF16)
        for half in range(2):
            for j in range(8):
                u_ref[pl.ds(pl.multiple_of(64 * (2 * p + half), 64), 64), 128 * j : 128 * j + 128] = u[
                    64 * j : 64 * j + 64, 128 * half : 128 * half + 128
                ]

        leave(p).start()

    def leave(p):
        rows = pl.ds(pl.multiple_of(128 * p, 128), 128)
        return pltpu.make_async_copy(u_ref.at[rows], out_ref.at[rows], sem.at[p])

    def statistics(p, u):
        for half in range(2):
            parts = [
                u[64 * half : 64 * half + 64, 128 * j : 128 * j + 128].astype(F32)
                for j in range(8)
            ]
            total = jnp.sum(sum(parts), axis=1, keepdims=True)
            mean = total * (1.0 / 1024)
            square = jnp.zeros((64, 128), F32)
            for part in parts:
                d = part - mean
                square = square + d * d
            here = lanes == 2 * p + half
            s1_ref[...] = jnp.where(here, total, s1_ref[...])
            m2_ref[...] = jnp.where(here, jnp.sum(square, axis=1, keepdims=True), m2_ref[...])

    convolve(0)

    def step(p, _):
        before = u_ref[pl.ds(pl.multiple_of(128 * p, 128), 128), :]
        convolve(p + 1)
        statistics(p, before)
        return 0

    pairs = u_ref.shape[0] // 128
    lax.fori_loop(0, pairs - 1, step, 0)
    statistics(pairs - 1, u_ref[128 * (pairs - 1) :, :])
    stats = jnp.concatenate([s1_ref[...], m2_ref[...]], axis=0).T[:16]

    def spread(s, _):
        stats_ref[s] = stats
        return 0

    lax.fori_loop(0, stats_ref.shape[0], spread, 0, unroll=8)
    for p in range(8):
        leave(p).wait()


def score_kernel(
    w_ref, x_ref, below_ref, above_ref, cbt_ref, _, out_ref, hot_ref, p_ref, taps_ref, t_ref, f_ref, sem
):
    count = x_ref.shape[3] // 128
    arrive = []
    for c in range(3):
        for z in range(2):
            inside = f_ref.at[c, 1 + z, :, pl.ds(128, 128 * count)]
            arrive.append(pltpu.make_async_copy(x_ref.at[c, z], inside, sem.at[2 * c + z]))
            arrive[-1].start()
    learners, sources = cbt_ref.shape
    entries = hot_ref.shape[1]
    live = jnp.where(cbt_ref[...] >= 0, 1.0, 0.0)
    earlier = lax.broadcasted_iota(jnp.int32, (learners, learners), 1) < lax.broadcasted_iota(
        jnp.int32, (learners, learners), 0
    )
    place = jnp.dot(
        jnp.where(earlier, 1.0, 0.0).astype(BF16), live.astype(BF16), preferred_element_type=F32
    )
    place = jnp.where(live > 0, place, -1.0).astype(BF16)
    lane = lax.broadcasted_iota(jnp.int32, (sources, entries), 1)
    start = SENT * lax.broadcasted_iota(jnp.int32, (sources, entries), 0)
    expand = jnp.where((lane >= start) & (lane < start + SENT), 1.0, 0.0).astype(BF16)
    wanted = jnp.dot(place, expand, preferred_element_type=F32)
    slot = (lax.broadcasted_iota(jnp.int32, (8, entries), 1) % SENT).astype(F32)[0:1]
    hot_ref[...] = jnp.where(wanted == slot, 1.0, 0.0).astype(BF16)
    load_params(w_ref, p_ref)
    fill_taps(p_ref, taps_ref)
    block = lane_iota() // 32
    zero = jnp.zeros((64, 128), F32)
    for zo in range(2):
        for yo in range(4):
            row = slice(64 * (4 * zo + yo), 64 * (4 * zo + yo) + 64)
            for c in range(3):
                edges = []
                for zz in range(4):
                    a = zz - zo
                    inside = 0 <= a <= 2
                    v = banded(taps_ref, c, a, yo) if inside else zero
                    col = 128 * (4 * c + zz)
                    t_ref[row, col : col + 128] = v.astype(BF16)
                    odd = zz % 2
                    if inside and yo == 0:
                        v = roll_lanes(taps_ref[c, a], 64 * odd)
                        edges.append(jnp.where(block == 2 * odd, v, 0.0))
                    elif inside and yo == 3:
                        v = roll_lanes(taps_ref[c, a], 64 * odd - 32)
                        edges.append(jnp.where(block == 2 * odd + 1, v, 0.0))
                    else:
                        edges.append(zero)
                for k in range(2):
                    col = 1536 + 128 * (2 * c + k)
                    v = edges[2 * k] + edges[2 * k + 1]
                    t_ref[row, col : col + 128] = v.astype(BF16)
    gain, shift, head, mean, var = (column(p_ref, k) for k in range(5))
    alpha = gain * lax.rsqrt(var + EPS)
    beta = shift - mean * alpha
    alpha = jnp.broadcast_to(alpha, (64, 128))
    beta = jnp.broadcast_to(beta, (64, 128))
    head = jnp.broadcast_to(head, (64, 128))

    empty = jnp.zeros((128, 128), BF16)
    for c in range(3):
        for zz in range(4):
            f_ref[c, zz, :, 0:128] = empty
            f_ref[c, zz, :, 128 * (count + 1) : 128 * (count + 2)] = empty

    def halo(b, _):
        src = pl.multiple_of(128 * b, 128)
        dst = pl.multiple_of(128 * b + 128, 128)
        for zz, ref in ((0, below_ref), (3, above_ref)):
            v = ref[0, :, pl.ds(src, 128)].astype(F32)
            for c, w in enumerate(shifted(v)):
                f_ref[c, zz, :, pl.ds(dst, 128)] = w.astype(BF16)
        return 0

    lax.fori_loop(0, count, halo, 0)
    for copy in arrive:
        copy.wait()

    def step(p, _):
        at = pl.multiple_of(256 * p, 128)
        pairs = [(c, zz) for c in range(3) for zz in range(4)]
        rows = [f_ref[c, zz, :, pl.ds(at + 128, 256)] for c, zz in pairs]
        for c, zz in pairs:
            rows.append(f_ref[c, zz, 96:128, pl.ds(at, 256)])
            rows.append(f_ref[c, zz, 0:32, pl.ds(at + 256, 256)])
        out = jnp.dot(t_ref[...], jnp.concatenate(rows, axis=0), preferred_element_type=F32)
        for half in range(2):
            for j in range(8):
                v = out[64 * j : 64 * j + 64, 128 * half : 128 * half + 128]
                h = jnp.maximum(v * alpha + beta, 0.0) * head
                out_ref[j // 4, 2 * p + half, j % 4 : j % 4 + 1, :] = jnp.sum(
                    h, axis=0, keepdims=True
                )
        return 0

    lax.fori_loop(0, count // 2, step, 0)


def exact_dot(a, v):
    hi = v.astype(BF16)
    rest = v - hi.astype(F32)
    mid = rest.astype(BF16)
    low = (rest - mid.astype(F32)).astype(BF16)
    out = jnp.dot(a, low, preferred_element_type=F32)
    out = out + jnp.dot(a, mid, preferred_element_type=F32)
    return out + jnp.dot(a, hi, preferred_element_type=F32)


def learner_kernel(
    cb_ref, w_ref, r_ref, cbt_ref, u_in_ref, lab_ref,
    send_out_ref, g_out_ref, mr_ref, vec_ref, inv_ref, row_ref,
    p_ref, acc_ref, part_ref, coef_ref, scale_ref, al_ref, be_ref, hd_ref, r0_ref, ru_ref,
    u_ref, send_ref, g_ref, sem,
):
    arrive = pltpu.make_async_copy(u_in_ref, u_ref, sem.at[0])
    arrive.start()
    load_params(w_ref, p_ref)
    lanes = lane_iota()
    learners, sources = cbt_ref.shape
    entries = r_ref.shape[0]
    lane = lax.broadcasted_iota(jnp.int32, (sources, entries), 1)
    source = lax.broadcasted_iota(jnp.int32, (sources, entries), 0)
    expand = jnp.where(lane // 16 == source, 1.0, 0.0).astype(BF16)
    wanted = jnp.dot(cbt_ref[...].astype(BF16), expand, preferred_element_type=F32)
    which = lax.broadcasted_iota(jnp.int32, (learners, entries), 1) % 16
    onehot = jnp.where(wanted == which.astype(F32), 1.0, 0.0).astype(BF16)
    number = jnp.sum(jnp.where(cbt_ref[...] >= 0, 1.0, 0.0), axis=1, keepdims=True)
    r = r_ref[...]
    means = r * (1.0 / 1024)
    centre = jnp.mean(means, axis=0, keepdims=True)
    d = means - centre
    rolled = pltpu.roll(d, 64, 1)
    low_half = lax.broadcasted_iota(jnp.int32, (entries, 128), 1) < 64
    v = jnp.where(low_half, d, means + rolled * rolled)
    p = exact_dot(onehot, v) / number
    first = jnp.where(lanes < 64, p, 0.0)
    mu = first + centre
    var = pltpu.roll(p, 64, 1) - first * first
    rstd = lax.rsqrt(jnp.maximum(var, 0.0) + EPS)
    both = jnp.where(lanes < 64, mu, pltpu.roll(rstd, 64, 1))
    both_t = jnp.concatenate([both, jnp.zeros((128 - learners, 128), F32)], axis=0).T
    mr_ref[...] = both_t
    inverse = jnp.broadcast_to(1.0 / (number * 1024.0), (learners, 128))
    inverse = jnp.concatenate([inverse, jnp.zeros((128 - learners, 128), F32)], axis=0).T
    inv_ref[...] = inverse[:8]
    row_ref[...] = jnp.full((8, 128), -1, jnp.int32)
    gain, shift, head = (jnp.broadcast_to(column(p_ref, k), (64, 128)) for k in range(3))
    alpha = gain * both_t[64:]
    al_ref[...] = alpha
    be_ref[...] = shift - alpha * both_t[:64]
    hd_ref[...] = head
    r0_ref[...] = jnp.zeros((64, 128), F32)
    ru_ref[...] = jnp.zeros((64, 128), F32)
    acc_ref[...] = jnp.zeros_like(acc_ref)
    part_ref[...] = jnp.zeros_like(part_ref)
    live = cb_ref[2 * learners]
    arrive.wait()

    def reduce(k, e):
        here = lanes == k
        r0 = jnp.sum(part_ref[2 * e], axis=1, keepdims=True)
        rh = jnp.sum(part_ref[2 * e + 1], axis=1, keepdims=True)
        r0_ref[...] = jnp.where(here, r0, r0_ref[...])
        ru_ref[...] = jnp.where(here, rh, ru_ref[...])

    def fetch(k):
        t = cb_ref[jnp.minimum(k, live - 1)]
        index = jnp.full((64, 128), t, jnp.int32)
        inv = jnp.take_along_axis(inv_ref[...], index[:8], axis=1)
        al = jnp.take_along_axis(al_ref[...], index, axis=1)
        be = jnp.take_along_axis(be_ref[...], index, axis=1)
        return jnp.where(k < live, inv, 0.0), al, be, hd_ref[...] * al

    def keep(e, coefficients):
        scale_ref[e] = coefficients[0]
        for n in range(3):
            coef_ref[3 * e + n] = coefficients[1 + n]

    def learner(k, e):
        t = cb_ref[jnp.minimum(k, live - 1)]
        b = cb_ref[learners + t]
        at = pl.multiple_of(b * 128, 128)
        row = pl.multiple_of(b * 64, 64)
        row_ref[...] = jnp.where(lanes[:8] == t, b, row_ref[...])
        al, be, c1 = (coef_ref[3 * e + n] for n in range(3))
        inv = scale_ref[e, 0:1]
        hd = hd_ref[...]
        r0 = jnp.zeros((64, 128), F32)
        rh = jnp.zeros((64, 128), F32)
        for j in range(8):
            us = u_ref[pl.ds(row, 64), 128 * j : 128 * j + 128].astype(F32)
            h = jnp.maximum(us * al + be, 0.0)
            score = jnp.sum(h * hd, axis=0, keepdims=True)
            res = (score - lab_ref[b, j : j + 1, :]) * inv
            m = jnp.where(h > 0, res, 0.0)
            r0 = r0 + m
            rh = rh + h * res
            acc_ref[64 * j : 64 * j + 64, pl.ds(at, 128)] += c1 * m
        part_ref[2 * e] = r0
        part_ref[2 * e + 1] = rh

    def step(i, _):
        for e in range(2):
            reduce(2 * i - 2 + e, e)
        following = [fetch(2 * i + 2 + e) for e in range(2)]
        for e in range(2):
            learner(2 * i + e, e)
            keep(e, following[e])
        return 0

    for e in range(2):
        keep(e, fetch(e))
    steps = (live + 1) // 2
    lax.fori_loop(0, steps, step, 0)
    for e in range(2):
        reduce(2 * steps - 2 + e, e)
    r0 = r0_ref[...]
    r1 = (ru_ref[...] - shift * r0) / gain
    sends = send_ref.shape[1]
    out = jnp.concatenate([r0, r1], axis=0).T[:sends].astype(BF16)

    def spread(s, _):
        send_ref[s] = out
        return 0

    lax.fori_loop(0, send_ref.shape[0], spread, 0, unroll=8)
    send = pltpu.make_async_copy(send_ref, send_out_ref, sem.at[1])
    send.start()
    leaves = []
    for j in range(8):
        rows = slice(64 * j, 64 * j + 64)
        g_ref[rows, :] = acc_ref[rows, :].astype(BF16)
        leaves.append(pltpu.make_async_copy(g_ref.at[rows], g_out_ref.at[rows], sem.at[2 + j]))
        leaves[j].start()
    dgain = jnp.sum(head * r1, axis=1, keepdims=True)
    dshift = jnp.sum(head * r0, axis=1, keepdims=True)
    dhead = jnp.sum(gain * r1 + shift * r0, axis=1, keepdims=True)
    vec_ref[...] = jnp.where(
        lanes == 96, dgain, jnp.where(lanes == 97, dshift, jnp.where(lanes == 98, dhead, 0.0))
    )
    send.wait()
    for leave in leaves:
        leave.wait()


def gradient_kernel(
    w_ref, r_ref, hot_ref, mr_ref, inv_ref, cb_ref, vec_ref, g_in_ref, u_in_ref, x_in_ref,
    out_ref, p_ref, full_ref, dt_ref, row_ref, g_ref, u_ref, x_ref, sem,
):
    arrive = [
        pltpu.make_async_copy(g_in_ref, g_ref, sem.at[0]),
        pltpu.make_async_copy(u_in_ref, u_ref, sem.at[1]),
    ]
    arrive += [pltpu.make_async_copy(x_in_ref.at[c], x_ref.at[c], sem.at[2 + c]) for c in range(3)]
    for copy in arrive:
        copy.start()
    load_params(w_ref, p_ref)
    learners = hot_ref.shape[0]
    total = jnp.dot(hot_ref[...], r_ref[...], preferred_element_type=F32)
    total = jnp.concatenate([total, jnp.zeros((128 - learners, 128), F32)], axis=0).T
    gain, head = (jnp.broadcast_to(column(p_ref, k), (64, 128)) for k in (0, 2))
    factor = gain * head * inv_ref[0:1, :]
    first = factor * total[:64]
    second = factor * total[64:]
    mu = mr_ref[:64]
    rstd = mr_ref[64:]
    slope = rstd * rstd * second
    offset = rstd * first - slope * mu
    row = cb_ref[0:1, :]

    def block(b, _):
        at = pl.multiple_of(b * 128, 128)
        row64 = pl.multiple_of(b * 64, 64)
        here = row == b
        e = jnp.broadcast_to(jnp.sum(jnp.where(here, offset, 0.0), axis=1, keepdims=True), (64, 128))
        f = jnp.broadcast_to(jnp.sum(jnp.where(here, slope, 0.0), axis=1, keepdims=True), (64, 128))
        for j in range(8):
            rows = slice(64 * j, 64 * j + 64)
            v = g_ref[rows, pl.ds(at, 128)].astype(F32) - e
            v = v - f * u_ref[pl.ds(row64, 64), 128 * j : 128 * j + 128].astype(F32)
            full_ref[rows, pl.ds(at, 128)] = v.astype(BF16)
        return 0

    arrive[0].wait()
    arrive[1].wait()
    lax.fori_loop(0, 16, block, 0)
    for c in range(3):
        arrive[2 + c].wait()
        dt_ref[:, 256 * c : 256 * c + 256] = lax.dot_general(
            full_ref[...],
            jnp.concatenate([x_ref[c, 0], x_ref[c, 1]], axis=0),
            (((1,), (1,)), ((), ())),
            preferred_element_type=F32,
        )
    blocks = lane_iota() // 32
    outs = [jnp.zeros((64, 128), F32) for _ in range(6)] + [vec_ref[...]]
    for c in range(3):
        for a in range(3):
            acc = jnp.zeros((64, 128), F32)
            for zo in range(2):
                z = zo + a - 1
                if not 0 <= z <= 1:
                    continue
                for yo in range(4):
                    j = 4 * zo + yo
                    col = 256 * c + 128 * z
                    v = roll_lanes(dt_ref[64 * j : 64 * j + 64, col : col + 128], -32 * (yo - 1))
                    if yo == 0:
                        v = jnp.where(blocks == 0, 0.0, v)
                    if yo == 3:
                        v = jnp.where(blocks == 2, 0.0, v)
                    acc = acc + v
            for b in range(3):
                tap = 9 * a + 3 * b + c
                k = tap // 4
                outs[k] = jnp.where(
                    blocks == tap % 4, roll_lanes(acc, 32 * (tap % 4 - b)), outs[k]
                )
    outs.append(jnp.zeros((64, 128), F32))
    for k in range(8):
        row_ref[pl.ds(k, 64, stride=8), :] = outs[k]
    packed = row_ref[...].astype(BF16)
    for role in range(out_ref.shape[0] // 512):
        out_ref[512 * role : 512 * role + 512, :] = packed


def finish_kernel(r_ref, weight_ref, vector_ref):
    total = jnp.sum(r_ref[...].astype(F32), axis=0)
    for k in range(6):
        weight_ref[:, 128 * k : 128 * k + 128] = total[k : k + 1]
    weight_ref[:, 768:864] = total[6:7, :96]
    vector_ref[...] = total[6:7, 96:99]


def per_device(features, labels, crop_block, weight, gain, shift, head, run_mean, run_var):
    devices = lax.axis_size("dev")
    roles = lax.axis_size("role")
    row = jnp.pad(weight, ((0, 0), (0, 896 - 864)))
    vectors = jnp.concatenate([gain, shift, head, run_mean, run_var])
    row = row + jnp.pad(vectors[None], ((0, 0), (864, 27)))
    rows = pl.pallas_call(
        pack_kernel,
        out_shape=jax.ShapeDtypeStruct((devices, 8, 128), BF16),
        in_specs=[VMEM],
        out_specs=VMEM,
        compiler_params=SMALL,
        name="pack",
    )(row)
    params = near(lax.all_to_all(rows, "dev", 0, 0, tiled=True))

    slab = features[0]
    channels, planes, height, columns = slab.shape
    count = height // CY
    cells = count * columns
    field = pl.pallas_call(
        prep_kernel,
        out_shape=pltpu.VMEM((3, planes, CY * channels, cells), BF16),
        grid=(planes,),
        in_specs=[pl.BlockSpec((channels, 1, height, columns), lambda z: (0, z, 0, 0))],
        out_specs=pl.BlockSpec((3, 1, CY * channels, cells), lambda z: (0, z, 0, 0)),
        scratch_shapes=[pltpu.VMEM((channels * height, columns), F32)],
        cost_estimate=pl.CostEstimate(flops=10**7, bytes_accessed=4 << 20, transcendentals=0),
        compiler_params=SMALL,
        name="prep",
    )(slab)

    targets = labels[0].reshape(planes, count, CY, columns).transpose(1, 0, 2, 3)
    targets = targets.reshape(count, planes * CY, columns).astype(F32)

    u, stats = pl.pallas_call(
        crop_conv_kernel,
        out_shape=(
            pltpu.HBM((64 * count, 1024), BF16),
            pltpu.HBM((devices, count, 128), F32),
        ),
        in_specs=[VMEM] * 2,
        out_specs=(HBM, VMEM),
        scratch_shapes=[
            PARAMS,
            pltpu.VMEM((3, 3, 64, 128), F32),
            pltpu.VMEM((512, 768), BF16),
            pltpu.VMEM((64, 128), F32),
            pltpu.VMEM((64, 128), F32),
            pltpu.VMEM((64 * count, 1024), BF16),
            DMA((8,)),
        ],
        cost_estimate=pl.CostEstimate(flops=2 * 512 * 768 * cells, bytes_accessed=8 << 20, transcendentals=0),
        compiler_params=SMALL,
        name="crop_conv",
    )(params, near(field))

    table, _ = lax.optimization_barrier((crop_block[0], stats))
    own_index = lax.axis_index("dev")
    mine = lax.dynamic_slice_in_dim(table, own_index, 1, 0)[0]
    live = mine >= 0
    places = jnp.arange(devices)
    before = jnp.sum(live[None, :] & (places[None, :] < places[:, None]), axis=1)
    at = live[None, :] & (before[None, :] == places[:, None])
    order = jnp.sum(jnp.where(at, places[None, :], 0), axis=1)
    lists = jnp.concatenate([order, mine, jnp.sum(live.astype(jnp.int32))[None]]).astype(jnp.int32)
    turned = table.T.astype(F32)
    gathered = lax.all_to_all(stats, "dev", 0, 0, tiled=True)
    gathered = gathered.reshape(devices * count, 128)
    plane = field[1]
    below = lax.ppermute(plane[-1:], "dev", [(i, i + 1) for i in range(devices - 1)])
    above = lax.ppermute(plane[:1], "dev", [(i + 1, i) for i in range(devices - 1)])

    send, g, mr, vec, inverse, mine_row = pl.pallas_call(
        learner_kernel,
        out_shape=(
            pltpu.HBM((devices, SENT, 128), BF16),
            pltpu.HBM((512, cells), BF16),
            jax.ShapeDtypeStruct((128, 128), F32),
            jax.ShapeDtypeStruct((64, 128), F32),
            jax.ShapeDtypeStruct((8, 128), F32),
            jax.ShapeDtypeStruct((8, 128), jnp.int32),
        ),
        in_specs=[SMEM] + [VMEM] * 3 + [HBM, VMEM],
        out_specs=(HBM, HBM) + (VMEM,) * 4,
        scratch_shapes=[
            PARAMS,
            pltpu.VMEM((512, cells), F32),
            pltpu.VMEM((4, 64, 128), F32),
            pltpu.VMEM((6, 64, 128), F32),
            pltpu.VMEM((2, 8, 128), F32),
        ]
        + [pltpu.VMEM((64, 128), F32)] * 5
        + [
            pltpu.VMEM((64 * count, 1024), BF16),
            pltpu.VMEM((devices, SENT, 128), BF16),
            pltpu.VMEM((512, cells), BF16),
            DMA((10,)),
        ],
        cost_estimate=pl.CostEstimate(flops=10**10, bytes_accessed=8 << 20, transcendentals=0),
        compiler_params=SMALL,
        name="learner",
    )(lists, params, near(gathered), turned, far(u), targets)

    arrived = lax.all_to_all(send, "dev", 0, 0, tiled=True)

    scores, hot = pl.pallas_call(
        score_kernel,
        out_shape=(
            jax.ShapeDtypeStruct((planes, count, CY, columns), F32),
            pltpu.VMEM((devices, devices * SENT), BF16),
        ),
        in_specs=[VMEM, HBM] + [VMEM] * 3 + [ANY],
        out_specs=(VMEM, VMEM),
        scratch_shapes=[
            PARAMS,
            pltpu.VMEM((3, 3, 64, 128), F32),
            pltpu.VMEM((512, 2304), BF16),
            pltpu.VMEM((3, planes + 2, CY * channels, cells + 256), BF16),
            DMA((6,)),
        ],
        cost_estimate=pl.CostEstimate(flops=2 * 512 * 2304 * cells, bytes_accessed=8 << 20, transcendentals=0),
        compiler_params=SMALL,
        name="score",
    )(params, far(field), below, above, turned, vec)

    final = pl.pallas_call(
        gradient_kernel,
        out_shape=jax.ShapeDtypeStruct((roles * devices * 8, 128), BF16),
        in_specs=[VMEM] * 7 + [HBM] * 3,
        out_specs=VMEM,
        scratch_shapes=[
            PARAMS,
            pltpu.VMEM((512, cells), BF16),
            pltpu.VMEM((512, 768), F32),
            pltpu.VMEM((512, 128), F32),
            pltpu.VMEM((512, cells), BF16),
            pltpu.VMEM((64 * count, 1024), BF16),
            pltpu.VMEM((3, planes, CY * channels, cells), BF16),
            DMA((5,)),
        ],
        cost_estimate=pl.CostEstimate(flops=2 * 512 * 768 * cells, bytes_accessed=8 << 20, transcendentals=0),
        compiler_params=SMALL,
        name="gradient",
    )(
        params,
        near(arrived.reshape(devices * SENT, 128)),
        near(hot), mr, inverse, mine_row, vec, far(g), far(u), far(field),
    )
    final = lax.all_to_all(
        final.reshape(roles * devices, 8, 128), ("role", "dev"), 0, 0, tiled=True
    )
    weight_grad, vector_grad = pl.pallas_call(
        finish_kernel,
        out_shape=(
            jax.ShapeDtypeStruct((1, 864), F32),
            jax.ShapeDtypeStruct((1, 3), F32),
        ),
        in_specs=[VMEM],
        out_specs=(VMEM, VMEM),
        compiler_params=SMALL,
        name="finish",
    )(near(final))
    return (scores.reshape(1, planes, height, columns), weight_grad, vector_grad)


def solution(mesh):
    in_specs = (
        P("role", None, "dev", None, None),
        P("role", "dev", None, None),
        P("role", None, None),
        P("dev", None),
        P("dev"),
        P("dev"),
        P("dev"),
        P("dev"),
        P("dev"),
    )
    out_specs = (P("role", "dev", None, None), P("dev", None), P("dev", None))
    return jax.shard_map(
        per_device, mesh=mesh, in_specs=in_specs, out_specs=out_specs, check_vma=False
    )
```

```python
import jax
import jax.numpy as jnp
from jax import lax
from jax.experimental import pallas as pl
from jax.experimental.pallas import tpu as pltpu
from jax.sharding import PartitionSpec as P


CY = 4
EPS = 1e-05
SENT = 48
F32 = jnp.float32
BF16 = jnp.bfloat16
PARAMS = pltpu.VMEM((512, 128), F32)
VMEM = pl.BlockSpec(memory_space=pltpu.VMEM)
SMALL = pltpu.CompilerParams(vmem_limit_bytes=20 << 20)
HBM = pl.BlockSpec(memory_space=pltpu.HBM)
DMA = pltpu.SemaphoreType.DMA
SMEM = pl.BlockSpec(memory_space=pltpu.SMEM)


def near(x):
    return pltpu.with_memory_space_constraint(x, pltpu.VMEM)


def far(x):
    return pltpu.with_memory_space_constraint(x, pltpu.HBM)


def lane_iota(rows=64):
    return lax.broadcasted_iota(jnp.int32, (rows, 128), 1)


def roll_lanes(x, shift):
    shift %= 128
    return x if shift == 0 else pltpu.roll(x, shift, 1)


def load_params(w_ref, p_ref):
    wide = w_ref[...].astype(F32)
    p_ref[...] = wide.reshape(wide.shape[0] * 8, 128)


def chunk(p_ref, k):
    return p_ref[pl.ds(k, 64, stride=8), :]


def column(v_ref, k):
    return v_ref[:, k : k + 1]


def fill_taps(p_ref, taps_ref):
    block = lane_iota() // 32
    chunks = [chunk(p_ref, k) for k in range(7)]
    for a in range(3):
        for c in range(3):
            out = jnp.zeros((64, 128), F32)
            for b in range(3):
                tap = 9 * a + 3 * b + c
                moved = roll_lanes(chunks[tap // 4], 32 * (b - tap % 4))
                out = jnp.where(block == b, moved, out)
            taps_ref[c, a] = out


def banded(taps_ref, c, a, yo):
    block = lane_iota() // 32
    v = roll_lanes(taps_ref[c, a], 32 * (yo - 1))
    if yo == 0:
        v = jnp.where(block == 3, 0.0, v)
    if yo == 3:
        v = jnp.where(block == 0, 0.0, v)
    return v


def pack_kernel(weight_ref, out_ref):
    sub = lax.broadcasted_iota(jnp.int32, (8, 128), 0)
    out = jnp.zeros((8, 128), F32)
    for k in range(6):
        out = jnp.where(sub == k, weight_ref[:, 128 * k : 128 * k + 128], out)
    tail = jnp.concatenate([weight_ref[:, 768:864], jnp.zeros((1, 32), F32)], axis=1)
    out = jnp.where(sub == 6, tail, out)
    out_ref[...] = jnp.broadcast_to(out.astype(BF16)[None], out_ref.shape)


def shifted(v):
    lane = lax.broadcasted_iota(jnp.int32, v.shape, 1)
    left = jnp.where(lane == 0, 0.0, pltpu.roll(v, 1, 1))
    right = jnp.where(lane == 127, 0.0, pltpu.roll(v, 127, 1))
    return left, v, right


def prep_kernel(slab_ref, x_ref, first_ref, last_ref, wide_ref, plane_ref, sem):
    channels, _, height, _ = slab_ref.shape
    wide_ref[...] = slab_ref[:, 0].astype(F32).reshape(channels * height, 128)
    for y in range(height):
        v = wide_ref[pl.ds(y, channels, stride=height), :]
        rows = slice(32 * (y % CY), 32 * (y % CY) + 32)
        lanes = slice(128 * (y // CY), 128 * (y // CY) + 128)
        for c, w in enumerate(shifted(v)):
            x_ref[c, 0, rows, lanes] = w.astype(BF16)
        plane_ref[pl.program_id(0), rows, lanes] = v.astype(BF16)
    last = pl.num_programs(0) - 1
    first_copy = pltpu.make_async_copy(plane_ref.at[0], first_ref.at[0], sem.at[0])
    last_copy = pltpu.make_async_copy(plane_ref.at[last], last_ref.at[0], sem.at[1])

    @pl.when(pl.program_id(0) == 0)
    def _():
        first_copy.start()

    @pl.when(pl.program_id(0) == last)
    def _():
        last_copy.start()
        first_copy.wait()
        last_copy.wait()


def crop_conv_kernel(
    gain_ref, shift_ref, head_ref, mean_ref, var_ref, w_ref, x_ref, out_ref, stats_ref, p_ref, taps_ref, t_ref, s1_ref, m2_ref, u_ref, sem
):
    load_params(w_ref, p_ref)
    fill_taps(p_ref, taps_ref)
    for zo in range(2):
        for yo in range(4):
            row = 64 * (4 * zo + yo)
            for c in range(3):
                for z in range(2):
                    col = 256 * c + 128 * z
                    v = banded(taps_ref, c, z - zo + 1, yo)
                    t_ref[row : row + 64, col : col + 128] = v.astype(BF16)
    s1_ref[...] = jnp.zeros((64, 128), F32)
    m2_ref[...] = jnp.zeros((64, 128), F32)
    lanes = lane_iota()

    def convolve(p):
        dst = pl.multiple_of(256 * p, 128)
        x = jnp.concatenate(
            [x_ref[c, z, :, pl.ds(dst, 256)] for c in range(3) for z in range(2)], axis=0
        )
        u = jnp.dot(t_ref[...], x, preferred_element_type=F32).astype(BF16)
        for half in range(2):
            for j in range(8):
                u_ref[pl.ds(pl.multiple_of(64 * (2 * p + half), 64), 64), 128 * j : 128 * j + 128] = u[
                    64 * j : 64 * j + 64, 128 * half : 128 * half + 128
                ]

        leave(p).start()

    def leave(p):
        rows = pl.ds(pl.multiple_of(128 * p, 128), 128)
        return pltpu.make_async_copy(u_ref.at[rows], out_ref.at[rows], sem.at[p])

    def statistics(p, u):
        for half in range(2):
            parts = [
                u[64 * half : 64 * half + 64, 128 * j : 128 * j + 128].astype(F32)
                for j in range(8)
            ]
            total = jnp.sum(sum(parts), axis=1, keepdims=True)
            mean = total * (1.0 / 1024)
            square = jnp.zeros((64, 128), F32)
            for part in parts:
                d = part - mean
                square = square + d * d
            here = lanes == 2 * p + half
            s1_ref[...] = jnp.where(here, total, s1_ref[...])
            m2_ref[...] = jnp.where(here, jnp.sum(square, axis=1, keepdims=True), m2_ref[...])

    convolve(0)

    def step(p, _):
        before = u_ref[pl.ds(pl.multiple_of(128 * p, 128), 128), :]
        convolve(p + 1)
        statistics(p, before)
        return 0

    pairs = u_ref.shape[0] // 128
    lax.fori_loop(0, pairs - 1, step, 0)
    statistics(pairs - 1, u_ref[128 * (pairs - 1) :, :])
    stat = jnp.concatenate([s1_ref[...], m2_ref[...]], axis=0).T[:16]
    low = lanes[:16] < 64
    high_term = stat.astype(BF16).astype(F32)
    top = jnp.where(low, high_term, pltpu.roll(stat - high_term, 64, 1))
    squares = jnp.where(low[:8], pltpu.roll(stat, 64, 1)[:8], stat[8:])
    sub = lax.broadcasted_iota(jnp.int32, (8, 128), 0)
    tail = jnp.zeros((8, 128), F32)
    for k, ref in enumerate((gain_ref, shift_ref, head_ref, mean_ref, var_ref)):
        tail = jnp.where((sub == 0) & (lanes[:8] == k), ref[0], tail)
    stats = jnp.concatenate([top, squares, tail], axis=0).astype(BF16)

    def spread(s, _):
        stats_ref[s] = stats
        return 0

    lax.fori_loop(0, stats_ref.shape[0], spread, 0, unroll=8)
    for p in range(8):
        leave(p).wait()


def score_kernel(
    w_ref, x_ref, below_ref, above_ref, cbt_ref, v_ref, out_ref, hot_ref, p_ref, taps_ref, t_ref, f_ref, sem
):
    count = x_ref.shape[3] // 128
    arrive = []
    for c in range(3):
        for z in range(2):
            inside = f_ref.at[c, 1 + z, :, pl.ds(128, 128 * count)]
            arrive.append(pltpu.make_async_copy(x_ref.at[c, z], inside, sem.at[2 * c + z]))
            arrive[-1].start()
    learners, sources = cbt_ref.shape
    entries = hot_ref.shape[1]
    live = jnp.where(cbt_ref[...] >= 0, 1.0, 0.0)
    earlier = lax.broadcasted_iota(jnp.int32, (learners, learners), 1) < lax.broadcasted_iota(
        jnp.int32, (learners, learners), 0
    )
    place = jnp.dot(
        jnp.where(earlier, 1.0, 0.0).astype(BF16), live.astype(BF16), preferred_element_type=F32
    )
    place = jnp.where(live > 0, place, -1.0).astype(BF16)
    lane = lax.broadcasted_iota(jnp.int32, (sources, entries), 1)
    start = SENT * lax.broadcasted_iota(jnp.int32, (sources, entries), 0)
    expand = jnp.where((lane >= start) & (lane < start + SENT), 1.0, 0.0).astype(BF16)
    wanted = jnp.dot(place, expand, preferred_element_type=F32)
    slot = (lax.broadcasted_iota(jnp.int32, (8, entries), 1) % SENT).astype(F32)[0:1]
    hot_ref[...] = jnp.where(wanted == slot, 1.0, 0.0).astype(BF16)
    load_params(w_ref, p_ref)
    fill_taps(p_ref, taps_ref)
    block = lane_iota() // 32
    zero = jnp.zeros((64, 128), F32)
    for zo in range(2):
        for yo in range(4):
            row = slice(64 * (4 * zo + yo), 64 * (4 * zo + yo) + 64)
            for c in range(3):
                edges = []
                for zz in range(4):
                    a = zz - zo
                    inside = 0 <= a <= 2
                    v = banded(taps_ref, c, a, yo) if inside else zero
                    col = 128 * (4 * c + zz)
                    t_ref[row, col : col + 128] = v.astype(BF16)
                    odd = zz % 2
                    if inside and yo == 0:
                        v = roll_lanes(taps_ref[c, a], 64 * odd)
                        edges.append(jnp.where(block == 2 * odd, v, 0.0))
                    elif inside and yo == 3:
                        v = roll_lanes(taps_ref[c, a], 64 * odd - 32)
                        edges.append(jnp.where(block == 2 * odd + 1, v, 0.0))
                    else:
                        edges.append(zero)
                for k in range(2):
                    col = 1536 + 128 * (2 * c + k)
                    v = edges[2 * k] + edges[2 * k + 1]
                    t_ref[row, col : col + 128] = v.astype(BF16)
    gain, shift, head, mean, var = (column(v_ref, k) for k in range(5))
    alpha = gain * lax.rsqrt(var + EPS)
    beta = shift - mean * alpha
    alpha = jnp.broadcast_to(alpha, (64, 128))
    beta = jnp.broadcast_to(beta, (64, 128))
    head = jnp.broadcast_to(head, (64, 128))

    empty = jnp.zeros((128, 128), BF16)
    for c in range(3):
        for zz in range(4):
            f_ref[c, zz, :, 0:128] = empty
            f_ref[c, zz, :, 128 * (count + 1) : 128 * (count + 2)] = empty

    def halo(b, _):
        src = pl.multiple_of(128 * b, 128)
        dst = pl.multiple_of(128 * b + 128, 128)
        for zz, ref in ((0, below_ref), (3, above_ref)):
            v = ref[0, :, pl.ds(src, 128)].astype(F32)
            for c, w in enumerate(shifted(v)):
                f_ref[c, zz, :, pl.ds(dst, 128)] = w.astype(BF16)
        return 0

    lax.fori_loop(0, count, halo, 0)
    for copy in arrive:
        copy.wait()

    def step(p, _):
        at = pl.multiple_of(256 * p, 128)
        pairs = [(c, zz) for c in range(3) for zz in range(4)]
        rows = [f_ref[c, zz, :, pl.ds(at + 128, 256)] for c, zz in pairs]
        for c, zz in pairs:
            rows.append(f_ref[c, zz, 96:128, pl.ds(at, 256)])
            rows.append(f_ref[c, zz, 0:32, pl.ds(at + 256, 256)])
        out = jnp.dot(t_ref[...], jnp.concatenate(rows, axis=0), preferred_element_type=F32)
        for half in range(2):
            for j in range(8):
                v = out[64 * j : 64 * j + 64, 128 * half : 128 * half + 128]
                h = jnp.maximum(v * alpha + beta, 0.0) * head
                out_ref[j // 4, 2 * p + half, j % 4 : j % 4 + 1, :] = jnp.sum(
                    h, axis=0, keepdims=True
                )
        return 0

    lax.fori_loop(0, count // 2, step, 0)


def exact_dot(a, v):
    hi = v.astype(BF16)
    rest = v - hi.astype(F32)
    mid = rest.astype(BF16)
    low = (rest - mid.astype(F32)).astype(BF16)
    out = jnp.dot(a, low, preferred_element_type=F32)
    out = out + jnp.dot(a, mid, preferred_element_type=F32)
    return out + jnp.dot(a, hi, preferred_element_type=F32)


def learner_kernel(
    cb_ref, r_ref, table_ref, u_in_ref, given_ref,
    send_out_ref, g_out_ref, mr_ref, vec_ref, inv_ref, row_ref, v_ref, cbt_ref,
    p_ref, acc_ref, part_ref, coef_ref, scale_ref, al_ref, be_ref, hd_ref, r0_ref, ru_ref,
    u_ref, send_ref, g_ref, lab_ref, sem,
):
    arrive = pltpu.make_async_copy(u_in_ref, u_ref, sem.at[0])
    arrive.start()
    cbt_ref[...] = table_ref[...].astype(F32).T
    given = given_ref[...].astype(F32)
    for b in range(lab_ref.shape[0]):
        lab_ref[b] = jnp.concatenate([given[z, CY * b : CY * b + CY] for z in range(2)], axis=0)
    lanes = lane_iota()
    learners, sources = cbt_ref.shape
    entries = sources * 16
    lane = lax.broadcasted_iota(jnp.int32, (sources, entries), 1)
    source = lax.broadcasted_iota(jnp.int32, (sources, entries), 0)
    expand = jnp.where(lane // 16 == source, 1.0, 0.0).astype(BF16)
    wanted = jnp.dot(cbt_ref[...].astype(BF16), expand, preferred_element_type=F32)
    which = lax.broadcasted_iota(jnp.int32, (learners, entries), 1) % 16
    onehot = jnp.where(wanted == which.astype(F32), 1.0, 0.0).astype(BF16)
    number = jnp.sum(jnp.where(cbt_ref[...] >= 0, 1.0, 0.0), axis=1, keepdims=True)
    wide = r_ref[...].astype(F32)
    low_half = lax.broadcasted_iota(jnp.int32, (entries, 128), 1) < 64
    top = wide[:, :16].reshape(entries, 128)
    squares = wide[:, 16:24]
    swapped = pltpu.roll(squares.reshape(sources * 8, 128), 64, 1).reshape(sources, 8, 128)
    squares = jnp.concatenate([swapped, squares], axis=1).reshape(entries, 128)
    r = jnp.where(low_half, top + pltpu.roll(top, 64, 1), squares)
    p_ref[...] = wide[:, 24:32].reshape(sources * 8, 128)
    v_ref[...] = p_ref[pl.ds(0, sources, stride=8), :]
    means = r * (1.0 / 1024)
    centre = jnp.mean(means, axis=0, keepdims=True)
    d = means - centre
    rolled = pltpu.roll(d, 64, 1)
    v = jnp.where(low_half, d, means + rolled * rolled)
    p = exact_dot(onehot, v) / number
    first = jnp.where(lanes < 64, p, 0.0)
    mu = first + centre
    var = pltpu.roll(p, 64, 1) - first * first
    rstd = lax.rsqrt(jnp.maximum(var, 0.0) + EPS)
    both = jnp.where(lanes < 64, mu, pltpu.roll(rstd, 64, 1))
    both_t = jnp.concatenate([both, jnp.zeros((128 - learners, 128), F32)], axis=0).T
    mr_ref[...] = both_t
    inverse = jnp.broadcast_to(1.0 / (number * 1024.0), (learners, 128))
    inverse = jnp.concatenate([inverse, jnp.zeros((128 - learners, 128), F32)], axis=0).T
    inv_ref[...] = inverse[:8]
    row_ref[...] = jnp.full((8, 128), -1, jnp.int32)
    gain, shift, head = (jnp.broadcast_to(column(v_ref, k), (64, 128)) for k in range(3))
    alpha = gain * both_t[64:]
    al_ref[...] = alpha
    be_ref[...] = shift - alpha * both_t[:64]
    hd_ref[...] = head
    r0_ref[...] = jnp.zeros((64, 128), F32)
    ru_ref[...] = jnp.zeros((64, 128), F32)
    acc_ref[...] = jnp.zeros_like(acc_ref)
    part_ref[...] = jnp.zeros_like(part_ref)
    live = cb_ref[2 * learners]
    arrive.wait()

    def reduce(k, e):
        here = lanes == k
        r0 = jnp.sum(part_ref[2 * e], axis=1, keepdims=True)
        rh = jnp.sum(part_ref[2 * e + 1], axis=1, keepdims=True)
        r0_ref[...] = jnp.where(here, r0, r0_ref[...])
        ru_ref[...] = jnp.where(here, rh, ru_ref[...])

    def fetch(k):
        t = cb_ref[jnp.minimum(k, live - 1)]
        index = jnp.full((64, 128), t, jnp.int32)
        inv = jnp.take_along_axis(inv_ref[...], index[:8], axis=1)
        al = jnp.take_along_axis(al_ref[...], index, axis=1)
        be = jnp.take_along_axis(be_ref[...], index, axis=1)
        return jnp.where(k < live, inv, 0.0), al, be, hd_ref[...] * al

    def keep(e, coefficients):
        scale_ref[e] = coefficients[0]
        for n in range(3):
            coef_ref[3 * e + n] = coefficients[1 + n]

    def learner(k, e):
        t = cb_ref[jnp.minimum(k, live - 1)]
        b = cb_ref[learners + t]
        row = pl.multiple_of(b * 64, 64)
        row_ref[...] = jnp.where(lanes[:8] == t, b, row_ref[...])
        al, be, c1 = (coef_ref[3 * e + n] for n in range(3))
        inv = scale_ref[e, 0:1]
        hd = hd_ref[...]
        r0 = jnp.zeros((64, 128), F32)
        rh = jnp.zeros((64, 128), F32)
        for j in range(8):
            us = u_ref[pl.ds(row, 64), 128 * j : 128 * j + 128].astype(F32)
            h = jnp.maximum(us * al + be, 0.0)
            score = jnp.sum(h * hd, axis=0, keepdims=True)
            res = (score - lab_ref[b, j : j + 1, :]) * inv
            m = jnp.where(h > 0, res, 0.0)
            r0 = r0 + m
            rh = rh + h * res
            acc_ref[pl.ds(row, 64), 128 * j : 128 * j + 128] += c1 * m
        part_ref[2 * e] = r0
        part_ref[2 * e + 1] = rh

    def step(i, _):
        for e in range(2):
            reduce(2 * i - 2 + e, e)
        following = [fetch(2 * i + 2 + e) for e in range(2)]
        for e in range(2):
            learner(2 * i + e, e)
            keep(e, following[e])
        return 0

    for e in range(2):
        keep(e, fetch(e))
    steps = (live + 1) // 2
    lax.fori_loop(0, steps, step, 0)
    for e in range(2):
        reduce(2 * steps - 2 + e, e)
    r0 = r0_ref[...]
    r1 = (ru_ref[...] - shift * r0) / gain
    sends = send_ref.shape[1]
    out = jnp.concatenate([r0, r1], axis=0).T[:sends].astype(BF16)

    def spread(s, _):
        send_ref[s] = out
        return 0

    lax.fori_loop(0, send_ref.shape[0], spread, 0, unroll=8)
    send = pltpu.make_async_copy(send_ref, send_out_ref, sem.at[1])
    send.start()
    leaves = []
    for j in range(8):
        rows = slice(128 * j, 128 * j + 128)
        g_ref[rows, :] = acc_ref[rows, :].astype(BF16)
        leaves.append(pltpu.make_async_copy(g_ref.at[rows], g_out_ref.at[rows], sem.at[2 + j]))
        leaves[j].start()
    dgain = jnp.sum(head * r1, axis=1, keepdims=True)
    dshift = jnp.sum(head * r0, axis=1, keepdims=True)
    dhead = jnp.sum(gain * r1 + shift * r0, axis=1, keepdims=True)
    vec_ref[...] = jnp.where(
        lanes == 96, dgain, jnp.where(lanes == 97, dshift, jnp.where(lanes == 98, dhead, 0.0))
    )
    send.wait()
    for leave in leaves:
        leave.wait()


def gradient_kernel(
    v_ref, r_ref, hot_ref, mr_ref, inv_ref, cb_ref, vec_ref, g_in_ref, u_in_ref, x_in_ref,
    out_ref, full_ref, dt_ref, row_ref, g_ref, u_ref, x_ref, sem,
):
    arrive = []
    for q in range(4):
        rows = pl.ds(256 * q, 256)
        arrive.append(pltpu.make_async_copy(g_in_ref.at[rows], g_ref.at[rows], sem.at[2 * q]))
        arrive.append(pltpu.make_async_copy(u_in_ref.at[rows], u_ref.at[rows], sem.at[2 * q + 1]))
    arrive += [pltpu.make_async_copy(x_in_ref.at[c], x_ref.at[c], sem.at[8 + c]) for c in range(3)]
    for copy in arrive:
        copy.start()
    learners = hot_ref.shape[0]
    total = jnp.dot(hot_ref[...], r_ref[...], preferred_element_type=F32)
    total = jnp.concatenate([total, jnp.zeros((128 - learners, 128), F32)], axis=0).T
    gain, head = (jnp.broadcast_to(column(v_ref, k), (64, 128)) for k in (0, 2))
    factor = gain * head * inv_ref[0:1, :]
    first = factor * total[:64]
    second = factor * total[64:]
    mu = mr_ref[:64]
    rstd = mr_ref[64:]
    slope = rstd * rstd * second
    offset = rstd * first - slope * mu
    row = cb_ref[0:1, :]

    def block(b, _):
        at = pl.multiple_of(b * 128, 128)
        row64 = pl.multiple_of(b * 64, 64)
        here = row == b
        e = jnp.broadcast_to(jnp.sum(jnp.where(here, offset, 0.0), axis=1, keepdims=True), (64, 128))
        f = jnp.broadcast_to(jnp.sum(jnp.where(here, slope, 0.0), axis=1, keepdims=True), (64, 128))
        for j in range(8):
            rows = slice(64 * j, 64 * j + 64)
            v = g_ref[pl.ds(row64, 64), 128 * j : 128 * j + 128].astype(F32) - e
            v = v - f * u_ref[pl.ds(row64, 64), 128 * j : 128 * j + 128].astype(F32)
            full_ref[rows, pl.ds(at, 128)] = v.astype(BF16)
        return 0

    for q in range(4):
        arrive[2 * q].wait()
        arrive[2 * q + 1].wait()
        lax.fori_loop(4 * q, 4 * q + 4, block, 0, unroll=2)
    for c in range(3):
        arrive[8 + c].wait()
        dt_ref[:, 256 * c : 256 * c + 256] = lax.dot_general(
            full_ref[...],
            jnp.concatenate([x_ref[c, 0], x_ref[c, 1]], axis=0),
            (((1,), (1,)), ((), ())),
            preferred_element_type=F32,
        )
    blocks = lane_iota() // 32
    outs = [jnp.zeros((64, 128), F32) for _ in range(6)] + [vec_ref[...]]
    for c in range(3):
        for a in range(3):
            acc = jnp.zeros((64, 128), F32)
            for zo in range(2):
                z = zo + a - 1
                if not 0 <= z <= 1:
                    continue
                for yo in range(4):
                    j = 4 * zo + yo
                    col = 256 * c + 128 * z
                    v = roll_lanes(dt_ref[64 * j : 64 * j + 64, col : col + 128], -32 * (yo - 1))
                    if yo == 0:
                        v = jnp.where(blocks == 0, 0.0, v)
                    if yo == 3:
                        v = jnp.where(blocks == 2, 0.0, v)
                    acc = acc + v
            for b in range(3):
                tap = 9 * a + 3 * b + c
                k = tap // 4
                outs[k] = jnp.where(
                    blocks == tap % 4, roll_lanes(acc, 32 * (tap % 4 - b)), outs[k]
                )
    outs.append(jnp.zeros((64, 128), F32))
    for k in range(8):
        row_ref[pl.ds(k, 64, stride=8), :] = outs[k]
    packed = row_ref[...].astype(BF16)
    for role in range(out_ref.shape[0] // 512):
        out_ref[512 * role : 512 * role + 512, :] = packed


def finish_kernel(r_ref, weight_ref, vector_ref):
    total = jnp.sum(r_ref[...].astype(F32), axis=0)
    for k in range(6):
        weight_ref[:, 128 * k : 128 * k + 128] = total[k : k + 1]
    weight_ref[:, 768:864] = total[6:7, :96]
    vector_ref[...] = total[6:7, 96:99]


def per_device(features, labels, crop_block, weight, gain, shift, head, run_mean, run_var):
    devices = lax.axis_size("dev")
    roles = lax.axis_size("role")
    rows = pl.pallas_call(
        pack_kernel,
        out_shape=jax.ShapeDtypeStruct((devices, 8, 128), BF16),
        in_specs=[VMEM],
        out_specs=VMEM,
        compiler_params=SMALL,
        name="pack",
    )(far(weight))
    params = near(lax.all_to_all(rows, "dev", 0, 0, tiled=True))

    slab = features[0]
    channels, planes, height, columns = slab.shape
    count = height // CY
    cells = count * columns
    field, first, last = pl.pallas_call(
        prep_kernel,
        out_shape=(
            pltpu.VMEM((3, planes, CY * channels, cells), BF16),
            pltpu.HBM((1, CY * channels, cells), BF16),
            pltpu.HBM((1, CY * channels, cells), BF16),
        ),
        grid=(planes,),
        in_specs=[pl.BlockSpec((channels, 1, height, columns), lambda z: (0, z, 0, 0))],
        out_specs=(
            pl.BlockSpec((3, 1, CY * channels, cells), lambda z: (0, z, 0, 0)),
            HBM,
            HBM,
        ),
        scratch_shapes=[
            pltpu.VMEM((channels * height, columns), F32),
            pltpu.VMEM((planes, CY * channels, cells), BF16),
            DMA((2,)),
        ],
        cost_estimate=pl.CostEstimate(flops=10**7, bytes_accessed=4 << 20, transcendentals=0),
        compiler_params=SMALL,
        name="prep",
    )(far(slab))

    *vectors, _ = lax.optimization_barrier((gain, shift, head, run_mean, run_var, field))
    u, stats = pl.pallas_call(
        crop_conv_kernel,
        out_shape=(
            pltpu.HBM((64 * count, 1024), BF16),
            pltpu.HBM((devices, 32, 128), BF16),
        ),
        in_specs=[SMEM] * 5 + [VMEM] * 2,
        out_specs=(HBM, VMEM),
        scratch_shapes=[
            PARAMS,
            pltpu.VMEM((3, 3, 64, 128), F32),
            pltpu.VMEM((512, 768), BF16),
            pltpu.VMEM((64, 128), F32),
            pltpu.VMEM((64, 128), F32),
            pltpu.VMEM((64 * count, 1024), BF16),
            DMA((8,)),
        ],
        cost_estimate=pl.CostEstimate(flops=2 * 512 * 768 * cells, bytes_accessed=8 << 20, transcendentals=0),
        compiler_params=SMALL,
        name="crop_conv",
    )(*vectors, params, near(field))

    table, _ = lax.optimization_barrier((crop_block[0], stats))
    own_index = lax.axis_index("dev")
    mine = lax.dynamic_slice_in_dim(table, own_index, 1, 0)[0]
    live = mine >= 0
    places = jnp.arange(devices)
    before = jnp.sum(live[None, :] & (places[None, :] < places[:, None]), axis=1)
    at = live[None, :] & (before[None, :] == places[:, None])
    order = jnp.sum(jnp.where(at, places[None, :], 0), axis=1)
    lists = jnp.concatenate([order, mine, jnp.sum(live.astype(jnp.int32))[None]]).astype(jnp.int32)
    gathered = lax.all_to_all(stats, "dev", 0, 0, tiled=True)
    below = lax.ppermute(last, "dev", [(i, i + 1) for i in range(devices - 1)])
    above = lax.ppermute(first, "dev", [(i + 1, i) for i in range(devices - 1)])

    send, g, mr, vec, inverse, mine_row, values, turned = pl.pallas_call(
        learner_kernel,
        out_shape=(
            pltpu.HBM((devices, SENT, 128), BF16),
            pltpu.HBM((64 * count, 1024), BF16),
            jax.ShapeDtypeStruct((128, 128), F32),
            jax.ShapeDtypeStruct((64, 128), F32),
            jax.ShapeDtypeStruct((8, 128), F32),
            jax.ShapeDtypeStruct((8, 128), jnp.int32),
            jax.ShapeDtypeStruct((64, 128), F32),
            jax.ShapeDtypeStruct((devices, devices), F32),
        ),
        in_specs=[SMEM] + [VMEM] * 2 + [HBM, VMEM],
        out_specs=(HBM, HBM) + (VMEM,) * 6,
        scratch_shapes=[
            PARAMS,
            pltpu.VMEM((64 * count, 1024), F32),
            pltpu.VMEM((4, 64, 128), F32),
            pltpu.VMEM((6, 64, 128), F32),
            pltpu.VMEM((2, 8, 128), F32),
        ]
        + [pltpu.VMEM((64, 128), F32)] * 5
        + [
            pltpu.VMEM((64 * count, 1024), BF16),
            pltpu.VMEM((devices, SENT, 128), BF16),
            pltpu.VMEM((64 * count, 1024), BF16),
            pltpu.VMEM((count, planes * CY, columns), F32),
            DMA((10,)),
        ],
        cost_estimate=pl.CostEstimate(flops=10**10, bytes_accessed=8 << 20, transcendentals=0),
        compiler_params=SMALL,
        name="learner",
    )(lists, near(gathered), table, far(u), labels[0])

    arrived = lax.all_to_all(send, "dev", 0, 0, tiled=True)

    scores, hot = pl.pallas_call(
        score_kernel,
        out_shape=(
            jax.ShapeDtypeStruct((planes, count, CY, columns), F32),
            pltpu.VMEM((devices, devices * SENT), BF16),
        ),
        in_specs=[VMEM, HBM] + [VMEM] * 4,
        out_specs=(VMEM, VMEM),
        scratch_shapes=[
            PARAMS,
            pltpu.VMEM((3, 3, 64, 128), F32),
            pltpu.VMEM((512, 2304), BF16),
            pltpu.VMEM((3, planes + 2, CY * channels, cells + 256), BF16),
            DMA((6,)),
        ],
        cost_estimate=pl.CostEstimate(flops=2 * 512 * 2304 * cells, bytes_accessed=8 << 20, transcendentals=0),
        compiler_params=SMALL,
        name="score",
    )(params, far(field), below, above, turned, values)

    final = pl.pallas_call(
        gradient_kernel,
        out_shape=jax.ShapeDtypeStruct((roles * devices * 8, 128), BF16),
        in_specs=[VMEM] * 7 + [HBM] * 3,
        out_specs=VMEM,
        scratch_shapes=[
            pltpu.VMEM((512, cells), BF16),
            pltpu.VMEM((512, 768), F32),
            pltpu.VMEM((512, 128), F32),
            pltpu.VMEM((64 * count, 1024), BF16),
            pltpu.VMEM((64 * count, 1024), BF16),
            pltpu.VMEM((3, planes, CY * channels, cells), BF16),
            DMA((11,)),
        ],
        cost_estimate=pl.CostEstimate(flops=2 * 512 * 768 * cells, bytes_accessed=8 << 20, transcendentals=0),
        compiler_params=SMALL,
        name="gradient",
    )(
        values,
        near(arrived.reshape(devices * SENT, 128)),
        near(hot), mr, inverse, mine_row, vec, far(g), far(u), far(field),
    )
    final = lax.all_to_all(
        final.reshape(roles * devices, 8, 128), ("role", "dev"), 0, 0, tiled=True
    )
    weight_grad, vector_grad = pl.pallas_call(
        finish_kernel,
        out_shape=(
            jax.ShapeDtypeStruct((1, 864), F32),
            jax.ShapeDtypeStruct((1, 3), F32),
        ),
        in_specs=[VMEM],
        out_specs=(VMEM, VMEM),
        compiler_params=SMALL,
        name="finish",
    )(near(final))
    return (scores.reshape(1, planes, height, columns), weight_grad, vector_grad)


def solution(mesh):
    in_specs = (
        P("role", None, "dev", None, None),
        P("role", "dev", None, None),
        P("role", None, None),
        P("dev", None),
        P("dev"),
        P("dev"),
        P("dev"),
        P("dev"),
        P("dev"),
    )
    out_specs = (P("role", "dev", None, None), P("dev", None), P("dev", None))
    return jax.shard_map(
        per_device, mesh=mesh, in_specs=in_specs, out_specs=out_specs, check_vma=False
    )
```

```python
import jax
import jax.numpy as jnp
from jax import lax
from jax.experimental import pallas as pl
from jax.experimental.pallas import tpu as pltpu
from jax.sharding import PartitionSpec as P


CY = 4
EPS = 1e-05
SENT = 48
F32 = jnp.float32
BF16 = jnp.bfloat16
PARAMS = pltpu.VMEM((512, 128), F32)
VMEM = pl.BlockSpec(memory_space=pltpu.VMEM)
SMALL = pltpu.CompilerParams(vmem_limit_bytes=20 << 20)
HBM = pl.BlockSpec(memory_space=pltpu.HBM)
DMA = pltpu.SemaphoreType.DMA
SMEM = pl.BlockSpec(memory_space=pltpu.SMEM)


def near(x):
    return pltpu.with_memory_space_constraint(x, pltpu.VMEM)


def far(x):
    return pltpu.with_memory_space_constraint(x, pltpu.HBM)


def lane_iota(rows=64):
    return lax.broadcasted_iota(jnp.int32, (rows, 128), 1)


def roll_lanes(x, shift):
    shift %= 128
    return x if shift == 0 else pltpu.roll(x, shift, 1)


def load_params(w_ref, p_ref):
    wide = w_ref[...].astype(F32)
    p_ref[...] = wide.reshape(wide.shape[0] * 8, 128)


def chunk(p_ref, k):
    return p_ref[pl.ds(k, 64, stride=8), :]


def column(v_ref, k):
    return v_ref[:, k : k + 1]


def fill_taps(p_ref, taps_ref):
    block = lane_iota() // 32
    chunks = [chunk(p_ref, k) for k in range(7)]
    for a in range(3):
        for c in range(3):
            out = jnp.zeros((64, 128), F32)
            for b in range(3):
                tap = 9 * a + 3 * b + c
                moved = roll_lanes(chunks[tap // 4], 32 * (b - tap % 4))
                out = jnp.where(block == b, moved, out)
            taps_ref[c, a] = out


def banded(taps_ref, c, a, yo):
    block = lane_iota() // 32
    v = roll_lanes(taps_ref[c, a], 32 * (yo - 1))
    if yo == 0:
        v = jnp.where(block == 3, 0.0, v)
    if yo == 3:
        v = jnp.where(block == 0, 0.0, v)
    return v


def pack_kernel(weight_ref, out_ref):
    sub = lax.broadcasted_iota(jnp.int32, (8, 128), 0)
    out = jnp.zeros((8, 128), F32)
    for k in range(6):
        out = jnp.where(sub == k, weight_ref[:, 128 * k : 128 * k + 128], out)
    tail = jnp.concatenate([weight_ref[:, 768:864], jnp.zeros((1, 32), F32)], axis=1)
    out = jnp.where(sub == 6, tail, out)
    out_ref[...] = jnp.broadcast_to(out.astype(BF16)[None], out_ref.shape)


def shifted(v):
    lane = lax.broadcasted_iota(jnp.int32, v.shape, 1)
    left = jnp.where(lane == 0, 0.0, pltpu.roll(v, 1, 1))
    right = jnp.where(lane == 127, 0.0, pltpu.roll(v, 127, 1))
    return left, v, right


def prep_kernel(slab_ref, x_ref, first_ref, last_ref, plane_ref, sem):
    channels, _, height, _ = slab_ref.shape
    to = lax.broadcasted_iota(jnp.int32, (256, 256), 0)
    source = lax.broadcasted_iota(jnp.int32, (256, 256), 1)
    exchange = (to // 16 == source % 16) & (to % 16 == source // 16)
    exchange = jnp.where(exchange, 1.0, 0.0).astype(BF16)
    for h in range(channels // 16):
        for g in range(height // 16):
            block = slab_ref[16 * h : 16 * h + 16, 0, 16 * g : 16 * g + 16, :]
            out = jnp.dot(exchange, block.reshape(256, 128), preferred_element_type=F32)
            for k in range(16):
                y = 16 * g + k
                v = out[16 * k : 16 * k + 16]
                rows = slice(32 * (y % CY) + 16 * h, 32 * (y % CY) + 16 * h + 16)
                lanes = slice(128 * (y // CY), 128 * (y // CY) + 128)
                for c, w in enumerate(shifted(v)):
                    x_ref[c, 0, rows, lanes] = w.astype(BF16)
                plane_ref[pl.program_id(0), rows, lanes] = v.astype(BF16)
    last = pl.num_programs(0) - 1
    first_copy = pltpu.make_async_copy(plane_ref.at[0], first_ref.at[0], sem.at[0])
    last_copy = pltpu.make_async_copy(plane_ref.at[last], last_ref.at[0], sem.at[1])

    @pl.when(pl.program_id(0) == 0)
    def _():
        first_copy.start()

    @pl.when(pl.program_id(0) == last)
    def _():
        last_copy.start()
        first_copy.wait()
        last_copy.wait()


def crop_conv_kernel(
    gain_ref, shift_ref, head_ref, mean_ref, var_ref, w_ref, x_ref, out_ref, stats_ref, p_ref, taps_ref, t_ref, s1_ref, m2_ref, u_ref, sem
):
    load_params(w_ref, p_ref)
    fill_taps(p_ref, taps_ref)
    for zo in range(2):
        for yo in range(4):
            row = 64 * (4 * zo + yo)
            for c in range(3):
                for z in range(2):
                    col = 256 * c + 128 * z
                    v = banded(taps_ref, c, z - zo + 1, yo)
                    t_ref[row : row + 64, col : col + 128] = v.astype(BF16)
    s1_ref[...] = jnp.zeros((64, 128), F32)
    m2_ref[...] = jnp.zeros((64, 128), F32)
    lanes = lane_iota()

    def convolve(p):
        dst = pl.multiple_of(256 * p, 128)
        x = jnp.concatenate(
            [x_ref[c, z, :, pl.ds(dst, 256)] for c in range(3) for z in range(2)], axis=0
        )
        u = jnp.dot(t_ref[...], x, preferred_element_type=F32).astype(BF16)
        for half in range(2):
            for j in range(8):
                u_ref[pl.ds(pl.multiple_of(64 * (2 * p + half), 64), 64), 128 * j : 128 * j + 128] = u[
                    64 * j : 64 * j + 64, 128 * half : 128 * half + 128
                ]

        leave(p).start()

    def leave(p):
        rows = pl.ds(pl.multiple_of(128 * p, 128), 128)
        return pltpu.make_async_copy(u_ref.at[rows], out_ref.at[rows], sem.at[p])

    def statistics(p, u):
        for half in range(2):
            parts = [
                u[64 * half : 64 * half + 64, 128 * j : 128 * j + 128].astype(F32)
                for j in range(8)
            ]
            total = jnp.sum(sum(parts), axis=1, keepdims=True)
            mean = total * (1.0 / 1024)
            square = jnp.zeros((64, 128), F32)
            for part in parts:
                d = part - mean
                square = square + d * d
            here = lanes == 2 * p + half
            s1_ref[...] = jnp.where(here, total, s1_ref[...])
            m2_ref[...] = jnp.where(here, jnp.sum(square, axis=1, keepdims=True), m2_ref[...])

    convolve(0)
    pairs = u_ref.shape[0] // 128
    for p in range(1, pairs):
        before = u_ref[128 * p - 128 : 128 * p, :]
        convolve(p)
        statistics(p - 1, before)
    statistics(pairs - 1, u_ref[128 * (pairs - 1) :, :])
    stat = jnp.concatenate([s1_ref[...], m2_ref[...]], axis=0).T[:16]
    low = lanes[:16] < 64
    high_term = stat.astype(BF16).astype(F32)
    top = jnp.where(low, high_term, pltpu.roll(stat - high_term, 64, 1))
    squares = jnp.where(low[:8], pltpu.roll(stat, 64, 1)[:8], stat[8:])
    sub = lax.broadcasted_iota(jnp.int32, (8, 128), 0)
    tail = jnp.zeros((8, 128), F32)
    for k, ref in enumerate((gain_ref, shift_ref, head_ref, mean_ref, var_ref)):
        tail = jnp.where((sub == 0) & (lanes[:8] == k), ref[0], tail)
    stats = jnp.concatenate([top, squares, tail], axis=0).astype(BF16)

    def spread(s, _):
        stats_ref[s] = stats
        return 0

    lax.fori_loop(0, stats_ref.shape[0], spread, 0, unroll=8)
    for p in range(8):
        leave(p).wait()


def score_kernel(
    w_ref, x_ref, below_ref, above_ref, cbt_ref, v_ref, out_ref, hot_ref, p_ref, taps_ref, t_ref, f_ref, sem
):
    count = x_ref.shape[3] // 128
    arrive = []
    for c in range(3):
        for z in range(2):
            inside = f_ref.at[c, 1 + z, :, pl.ds(128, 128 * count)]
            arrive.append(pltpu.make_async_copy(x_ref.at[c, z], inside, sem.at[2 * c + z]))
            arrive[-1].start()
    learners, sources = cbt_ref.shape
    entries = hot_ref.shape[1]
    live = jnp.where(cbt_ref[...] >= 0, 1.0, 0.0)
    earlier = lax.broadcasted_iota(jnp.int32, (learners, learners), 1) < lax.broadcasted_iota(
        jnp.int32, (learners, learners), 0
    )
    place = jnp.dot(
        jnp.where(earlier, 1.0, 0.0).astype(BF16), live.astype(BF16), preferred_element_type=F32
    )
    place = jnp.where(live > 0, place, -1.0).astype(BF16)
    lane = lax.broadcasted_iota(jnp.int32, (sources, entries), 1)
    start = SENT * lax.broadcasted_iota(jnp.int32, (sources, entries), 0)
    expand = jnp.where((lane >= start) & (lane < start + SENT), 1.0, 0.0).astype(BF16)
    wanted = jnp.dot(place, expand, preferred_element_type=F32)
    slot = (lax.broadcasted_iota(jnp.int32, (8, entries), 1) % SENT).astype(F32)[0:1]
    hot_ref[...] = jnp.where(wanted == slot, 1.0, 0.0).astype(BF16)
    load_params(w_ref, p_ref)
    fill_taps(p_ref, taps_ref)
    block = lane_iota() // 32
    zero = jnp.zeros((64, 128), F32)
    for zo in range(2):
        for yo in range(4):
            row = slice(64 * (4 * zo + yo), 64 * (4 * zo + yo) + 64)
            for c in range(3):
                edges = []
                for zz in range(4):
                    a = zz - zo
                    inside = 0 <= a <= 2
                    v = banded(taps_ref, c, a, yo) if inside else zero
                    col = 128 * (4 * c + zz)
                    t_ref[row, col : col + 128] = v.astype(BF16)
                    odd = zz % 2
                    if inside and yo == 0:
                        v = roll_lanes(taps_ref[c, a], 64 * odd)
                        edges.append(jnp.where(block == 2 * odd, v, 0.0))
                    elif inside and yo == 3:
                        v = roll_lanes(taps_ref[c, a], 64 * odd - 32)
                        edges.append(jnp.where(block == 2 * odd + 1, v, 0.0))
                    else:
                        edges.append(zero)
                for k in range(2):
                    col = 1536 + 128 * (2 * c + k)
                    v = edges[2 * k] + edges[2 * k + 1]
                    t_ref[row, col : col + 128] = v.astype(BF16)
    gain, shift, head, mean, var = (column(v_ref, k) for k in range(5))
    alpha = gain * lax.rsqrt(var + EPS)
    beta = shift - mean * alpha
    alpha = jnp.broadcast_to(alpha, (64, 128))
    beta = jnp.broadcast_to(beta, (64, 128))
    head = jnp.broadcast_to(head, (64, 128))

    empty = jnp.zeros((128, 128), BF16)
    for c in range(3):
        for zz in range(4):
            f_ref[c, zz, :, 0:128] = empty
            f_ref[c, zz, :, 128 * (count + 1) : 128 * (count + 2)] = empty

    def halo(b, _):
        src = pl.multiple_of(128 * b, 128)
        dst = pl.multiple_of(128 * b + 128, 128)
        for zz, ref in ((0, below_ref), (3, above_ref)):
            v = ref[0, :, pl.ds(src, 128)].astype(F32)
            for c, w in enumerate(shifted(v)):
                f_ref[c, zz, :, pl.ds(dst, 128)] = w.astype(BF16)
        return 0

    lax.fori_loop(0, count, halo, 0)
    for copy in arrive:
        copy.wait()

    def step(p, _):
        at = pl.multiple_of(256 * p, 128)
        pairs = [(c, zz) for c in range(3) for zz in range(4)]
        rows = [f_ref[c, zz, :, pl.ds(at + 128, 256)] for c, zz in pairs]
        for c, zz in pairs:
            rows.append(f_ref[c, zz, 96:128, pl.ds(at, 256)])
            rows.append(f_ref[c, zz, 0:32, pl.ds(at + 256, 256)])
        out = jnp.dot(t_ref[...], jnp.concatenate(rows, axis=0), preferred_element_type=F32)
        for half in range(2):
            for j in range(8):
                v = out[64 * j : 64 * j + 64, 128 * half : 128 * half + 128]
                h = jnp.maximum(v * alpha + beta, 0.0) * head
                out_ref[j // 4, 2 * p + half, j % 4 : j % 4 + 1, :] = jnp.sum(
                    h, axis=0, keepdims=True
                )
        return 0

    lax.fori_loop(0, count // 2, step, 0)


def exact_dot(a, v):
    hi = v.astype(BF16)
    rest = v - hi.astype(F32)
    mid = rest.astype(BF16)
    low = (rest - mid.astype(F32)).astype(BF16)
    out = jnp.dot(a, low, preferred_element_type=F32)
    out = out + jnp.dot(a, mid, preferred_element_type=F32)
    return out + jnp.dot(a, hi, preferred_element_type=F32)


def learner_kernel(
    cb_ref, r_ref, table_ref, u_in_ref, given_ref,
    send_out_ref, g_out_ref, mr_ref, vec_ref, inv_ref, row_ref, v_ref, cbt_ref,
    p_ref, acc_ref, part_ref, coef_ref, scale_ref, al_ref, be_ref, hd_ref, r0_ref, ru_ref,
    u_ref, send_ref, g_ref, lab_ref, sem,
):
    arrive = pltpu.make_async_copy(u_in_ref, u_ref, sem.at[0])
    arrive.start()
    cbt_ref[...] = table_ref[...].astype(F32).T
    given = given_ref[...].astype(F32)
    for b in range(lab_ref.shape[0]):
        lab_ref[b] = jnp.concatenate([given[z, CY * b : CY * b + CY] for z in range(2)], axis=0)
    lanes = lane_iota()
    learners, sources = cbt_ref.shape
    entries = sources * 16
    lane = lax.broadcasted_iota(jnp.int32, (sources, entries), 1)
    source = lax.broadcasted_iota(jnp.int32, (sources, entries), 0)
    expand = jnp.where(lane // 16 == source, 1.0, 0.0).astype(BF16)
    wanted = jnp.dot(cbt_ref[...].astype(BF16), expand, preferred_element_type=F32)
    which = lax.broadcasted_iota(jnp.int32, (learners, entries), 1) % 16
    onehot = jnp.where(wanted == which.astype(F32), 1.0, 0.0).astype(BF16)
    number = jnp.sum(jnp.where(cbt_ref[...] >= 0, 1.0, 0.0), axis=1, keepdims=True)
    wide = r_ref[...].astype(F32)
    low_half = lax.broadcasted_iota(jnp.int32, (entries, 128), 1) < 64
    top = wide[:, :16].reshape(entries, 128)
    squares = wide[:, 16:24]
    swapped = pltpu.roll(squares.reshape(sources * 8, 128), 64, 1).reshape(sources, 8, 128)
    squares = jnp.concatenate([swapped, squares], axis=1).reshape(entries, 128)
    r = jnp.where(low_half, top + pltpu.roll(top, 64, 1), squares)
    p_ref[...] = wide[:, 24:32].reshape(sources * 8, 128)
    v_ref[...] = p_ref[pl.ds(0, sources, stride=8), :]
    means = r * (1.0 / 1024)
    centre = jnp.mean(means, axis=0, keepdims=True)
    d = means - centre
    rolled = pltpu.roll(d, 64, 1)
    v = jnp.where(low_half, d, means + rolled * rolled)
    p = exact_dot(onehot, v) / number
    first = jnp.where(lanes < 64, p, 0.0)
    mu = first + centre
    var = pltpu.roll(p, 64, 1) - first * first
    rstd = lax.rsqrt(jnp.maximum(var, 0.0) + EPS)
    both = jnp.where(lanes < 64, mu, pltpu.roll(rstd, 64, 1))
    both_t = jnp.concatenate([both, jnp.zeros((128 - learners, 128), F32)], axis=0).T
    mr_ref[...] = both_t
    inverse = jnp.broadcast_to(1.0 / (number * 1024.0), (learners, 128))
    inverse = jnp.concatenate([inverse, jnp.zeros((128 - learners, 128), F32)], axis=0).T
    inv_ref[...] = inverse[:8]
    row_ref[...] = jnp.full((8, 128), -1, jnp.int32)
    gain, shift, head = (jnp.broadcast_to(column(v_ref, k), (64, 128)) for k in range(3))
    alpha = gain * both_t[64:]
    al_ref[...] = alpha
    be_ref[...] = shift - alpha * both_t[:64]
    hd_ref[...] = head
    r0_ref[...] = jnp.zeros((64, 128), F32)
    ru_ref[...] = jnp.zeros((64, 128), F32)
    acc_ref[...] = jnp.zeros_like(acc_ref)
    part_ref[...] = jnp.zeros_like(part_ref)
    live = cb_ref[2 * learners]
    arrive.wait()

    def reduce(k, e):
        here = lanes == k
        r0 = jnp.sum(part_ref[2 * e], axis=1, keepdims=True)
        rh = jnp.sum(part_ref[2 * e + 1], axis=1, keepdims=True)
        r0_ref[...] = jnp.where(here, r0, r0_ref[...])
        ru_ref[...] = jnp.where(here, rh, ru_ref[...])

    def fetch(k):
        t = cb_ref[jnp.minimum(k, live - 1)]
        index = jnp.full((64, 128), t, jnp.int32)
        inv = jnp.take_along_axis(inv_ref[...], index[:8], axis=1)
        al = jnp.take_along_axis(al_ref[...], index, axis=1)
        be = jnp.take_along_axis(be_ref[...], index, axis=1)
        return jnp.where(k < live, inv, 0.0), al, be, hd_ref[...] * al

    def keep(e, coefficients):
        scale_ref[e] = coefficients[0]
        for n in range(3):
            coef_ref[3 * e + n] = coefficients[1 + n]

    def learner(k, e):
        t = cb_ref[jnp.minimum(k, live - 1)]
        b = cb_ref[learners + t]
        row = pl.multiple_of(b * 64, 64)
        row_ref[...] = jnp.where(lanes[:8] == t, b, row_ref[...])
        al, be, c1 = (coef_ref[3 * e + n] for n in range(3))
        inv = scale_ref[e, 0:1]
        hd = hd_ref[...]
        r0 = jnp.zeros((64, 128), F32)
        rh = jnp.zeros((64, 128), F32)
        for j in range(8):
            us = u_ref[pl.ds(row, 64), 128 * j : 128 * j + 128].astype(F32)
            h = jnp.maximum(us * al + be, 0.0)
            score = jnp.sum(h * hd, axis=0, keepdims=True)
            res = (score - lab_ref[b, j : j + 1, :]) * inv
            m = jnp.where(h > 0, res, 0.0)
            r0 = r0 + m
            rh = rh + h * res
            acc_ref[pl.ds(row, 64), 128 * j : 128 * j + 128] += c1 * m
        part_ref[2 * e] = r0
        part_ref[2 * e + 1] = rh

    def step(i, _):
        for e in range(2):
            reduce(2 * i - 2 + e, e)
        following = [fetch(2 * i + 2 + e) for e in range(2)]
        for e in range(2):
            learner(2 * i + e, e)
            keep(e, following[e])
        return 0

    for e in range(2):
        keep(e, fetch(e))
    steps = (live + 1) // 2
    lax.fori_loop(0, steps, step, 0)
    for e in range(2):
        reduce(2 * steps - 2 + e, e)
    r0 = r0_ref[...]
    r1 = (ru_ref[...] - shift * r0) / gain
    sends = send_ref.shape[1]
    out = jnp.concatenate([r0, r1], axis=0).T[:sends].astype(BF16)

    def spread(s, _):
        send_ref[s] = out
        return 0

    lax.fori_loop(0, send_ref.shape[0], spread, 0, unroll=8)
    send = pltpu.make_async_copy(send_ref, send_out_ref, sem.at[1])
    send.start()
    leaves = []
    for j in range(8):
        rows = slice(128 * j, 128 * j + 128)
        g_ref[rows, :] = acc_ref[rows, :].astype(BF16)
        leaves.append(pltpu.make_async_copy(g_ref.at[rows], g_out_ref.at[rows], sem.at[2 + j]))
        leaves[j].start()
    dgain = jnp.sum(head * r1, axis=1, keepdims=True)
    dshift = jnp.sum(head * r0, axis=1, keepdims=True)
    dhead = jnp.sum(gain * r1 + shift * r0, axis=1, keepdims=True)
    vec_ref[...] = jnp.where(
        lanes == 96, dgain, jnp.where(lanes == 97, dshift, jnp.where(lanes == 98, dhead, 0.0))
    )
    send.wait()
    for leave in leaves:
        leave.wait()


def gradient_kernel(
    v_ref, r_ref, hot_ref, mr_ref, inv_ref, cb_ref, vec_ref, g_in_ref, u_in_ref, x_in_ref,
    out_ref, full_ref, dt_ref, row_ref, g_ref, u_ref, x_ref, sem,
):
    arrive = []
    for q in range(4):
        rows = pl.ds(256 * q, 256)
        arrive.append(pltpu.make_async_copy(g_in_ref.at[rows], g_ref.at[rows], sem.at[2 * q]))
        arrive.append(pltpu.make_async_copy(u_in_ref.at[rows], u_ref.at[rows], sem.at[2 * q + 1]))
    arrive += [pltpu.make_async_copy(x_in_ref.at[c], x_ref.at[c], sem.at[8 + c]) for c in range(3)]
    for copy in arrive:
        copy.start()
    learners = hot_ref.shape[0]
    total = jnp.dot(hot_ref[...], r_ref[...], preferred_element_type=F32)
    total = jnp.concatenate([total, jnp.zeros((128 - learners, 128), F32)], axis=0).T
    gain, head = (jnp.broadcast_to(column(v_ref, k), (64, 128)) for k in (0, 2))
    factor = gain * head * inv_ref[0:1, :]
    first = factor * total[:64]
    second = factor * total[64:]
    mu = mr_ref[:64]
    rstd = mr_ref[64:]
    slope = rstd * rstd * second
    offset = rstd * first - slope * mu
    row = cb_ref[0:1, :]

    def block(b, _):
        at = pl.multiple_of(b * 128, 128)
        row64 = pl.multiple_of(b * 64, 64)
        here = row == b
        e = jnp.broadcast_to(jnp.sum(jnp.where(here, offset, 0.0), axis=1, keepdims=True), (64, 128))
        f = jnp.broadcast_to(jnp.sum(jnp.where(here, slope, 0.0), axis=1, keepdims=True), (64, 128))
        for j in range(8):
            rows = slice(64 * j, 64 * j + 64)
            v = g_ref[pl.ds(row64, 64), 128 * j : 128 * j + 128].astype(F32) - e
            v = v - f * u_ref[pl.ds(row64, 64), 128 * j : 128 * j + 128].astype(F32)
            full_ref[rows, pl.ds(at, 128)] = v.astype(BF16)
        return 0

    for q in range(4):
        arrive[2 * q].wait()
        arrive[2 * q + 1].wait()
        lax.fori_loop(4 * q, 4 * q + 4, block, 0, unroll=4)
    for c in range(3):
        arrive[8 + c].wait()
        dt_ref[:, 256 * c : 256 * c + 256] = lax.dot_general(
            full_ref[...],
            jnp.concatenate([x_ref[c, 0], x_ref[c, 1]], axis=0),
            (((1,), (1,)), ((), ())),
            preferred_element_type=F32,
        )
    blocks = lane_iota() // 32
    outs = [jnp.zeros((64, 128), F32) for _ in range(6)] + [vec_ref[...]]
    for c in range(3):
        for a in range(3):
            acc = jnp.zeros((64, 128), F32)
            for zo in range(2):
                z = zo + a - 1
                if not 0 <= z <= 1:
                    continue
                for yo in range(4):
                    j = 4 * zo + yo
                    col = 256 * c + 128 * z
                    v = roll_lanes(dt_ref[64 * j : 64 * j + 64, col : col + 128], -32 * (yo - 1))
                    if yo == 0:
                        v = jnp.where(blocks == 0, 0.0, v)
                    if yo == 3:
                        v = jnp.where(blocks == 2, 0.0, v)
                    acc = acc + v
            for b in range(3):
                tap = 9 * a + 3 * b + c
                k = tap // 4
                outs[k] = jnp.where(
                    blocks == tap % 4, roll_lanes(acc, 32 * (tap % 4 - b)), outs[k]
                )
    outs.append(jnp.zeros((64, 128), F32))
    for k in range(8):
        row_ref[pl.ds(k, 64, stride=8), :] = outs[k]
    packed = row_ref[...].astype(BF16)
    for role in range(out_ref.shape[0] // 512):
        out_ref[512 * role : 512 * role + 512, :] = packed


def finish_kernel(r_ref, weight_ref, vector_ref):
    total = jnp.sum(r_ref[...].astype(F32), axis=0)
    for k in range(6):
        weight_ref[:, 128 * k : 128 * k + 128] = total[k : k + 1]
    weight_ref[:, 768:864] = total[6:7, :96]
    vector_ref[...] = total[6:7, 96:99]


def per_device(features, labels, crop_block, weight, gain, shift, head, run_mean, run_var):
    devices = lax.axis_size("dev")
    roles = lax.axis_size("role")
    rows = pl.pallas_call(
        pack_kernel,
        out_shape=jax.ShapeDtypeStruct((devices, 8, 128), BF16),
        in_specs=[VMEM],
        out_specs=VMEM,
        compiler_params=SMALL,
        name="pack",
    )(far(weight))
    params = near(lax.all_to_all(rows, "dev", 0, 0, tiled=True))

    slab = features[0]
    channels, planes, height, columns = slab.shape
    count = height // CY
    cells = count * columns
    field, first, last = pl.pallas_call(
        prep_kernel,
        out_shape=(
            pltpu.VMEM((3, planes, CY * channels, cells), BF16),
            pltpu.HBM((1, CY * channels, cells), BF16),
            pltpu.HBM((1, CY * channels, cells), BF16),
        ),
        grid=(planes,),
        in_specs=[pl.BlockSpec((channels, 1, height, columns), lambda z: (0, z, 0, 0))],
        out_specs=(
            pl.BlockSpec((3, 1, CY * channels, cells), lambda z: (0, z, 0, 0)),
            HBM,
            HBM,
        ),
        scratch_shapes=[
            pltpu.VMEM((planes, CY * channels, cells), BF16),
            DMA((2,)),
        ],
        cost_estimate=pl.CostEstimate(flops=10**7, bytes_accessed=4 << 20, transcendentals=0),
        compiler_params=SMALL,
        name="prep",
    )(far(slab))

    *vectors, _ = lax.optimization_barrier((gain, shift, head, run_mean, run_var, field))
    u, stats = pl.pallas_call(
        crop_conv_kernel,
        out_shape=(
            pltpu.HBM((64 * count, 1024), BF16),
            pltpu.HBM((devices, 32, 128), BF16),
        ),
        in_specs=[SMEM] * 5 + [VMEM] * 2,
        out_specs=(HBM, VMEM),
        scratch_shapes=[
            PARAMS,
            pltpu.VMEM((3, 3, 64, 128), F32),
            pltpu.VMEM((512, 768), BF16),
            pltpu.VMEM((64, 128), F32),
            pltpu.VMEM((64, 128), F32),
            pltpu.VMEM((64 * count, 1024), BF16),
            DMA((8,)),
        ],
        cost_estimate=pl.CostEstimate(flops=2 * 512 * 768 * cells, bytes_accessed=8 << 20, transcendentals=0),
        compiler_params=SMALL,
        name="crop_conv",
    )(*vectors, params, near(field))

    table, _ = lax.optimization_barrier((crop_block[0], stats))
    own_index = lax.axis_index("dev")
    mine = lax.dynamic_slice_in_dim(table, own_index, 1, 0)[0]
    live = mine >= 0
    places = jnp.arange(devices)
    before = jnp.sum(live[None, :] & (places[None, :] < places[:, None]), axis=1)
    at = live[None, :] & (before[None, :] == places[:, None])
    order = jnp.sum(jnp.where(at, places[None, :], 0), axis=1)
    lists = jnp.concatenate([order, mine, jnp.sum(live.astype(jnp.int32))[None]]).astype(jnp.int32)
    gathered = lax.all_to_all(stats, "dev", 0, 0, tiled=True)
    below = lax.ppermute(last, "dev", [(i, i + 1) for i in range(devices - 1)])
    above = lax.ppermute(first, "dev", [(i + 1, i) for i in range(devices - 1)])

    send, g, mr, vec, inverse, mine_row, values, turned = pl.pallas_call(
        learner_kernel,
        out_shape=(
            pltpu.HBM((devices, SENT, 128), BF16),
            pltpu.HBM((64 * count, 1024), BF16),
            jax.ShapeDtypeStruct((128, 128), F32),
            jax.ShapeDtypeStruct((64, 128), F32),
            jax.ShapeDtypeStruct((8, 128), F32),
            jax.ShapeDtypeStruct((8, 128), jnp.int32),
            jax.ShapeDtypeStruct((64, 128), F32),
            jax.ShapeDtypeStruct((devices, devices), F32),
        ),
        in_specs=[SMEM] + [VMEM] * 2 + [HBM, VMEM],
        out_specs=(HBM, HBM) + (VMEM,) * 6,
        scratch_shapes=[
            PARAMS,
            pltpu.VMEM((64 * count, 1024), F32),
            pltpu.VMEM((4, 64, 128), F32),
            pltpu.VMEM((6, 64, 128), F32),
            pltpu.VMEM((2, 8, 128), F32),
        ]
        + [pltpu.VMEM((64, 128), F32)] * 5
        + [
            pltpu.VMEM((64 * count, 1024), BF16),
            pltpu.VMEM((devices, SENT, 128), BF16),
            pltpu.VMEM((64 * count, 1024), BF16),
            pltpu.VMEM((count, planes * CY, columns), F32),
            DMA((10,)),
        ],
        cost_estimate=pl.CostEstimate(flops=10**10, bytes_accessed=8 << 20, transcendentals=0),
        compiler_params=SMALL,
        name="learner",
    )(lists, near(gathered), table, far(u), labels[0])

    arrived = lax.all_to_all(send, "dev", 0, 0, tiled=True)

    scores, hot = pl.pallas_call(
        score_kernel,
        out_shape=(
            jax.ShapeDtypeStruct((planes, count, CY, columns), F32),
            pltpu.VMEM((devices, devices * SENT), BF16),
        ),
        in_specs=[VMEM, HBM] + [VMEM] * 4,
        out_specs=(VMEM, VMEM),
        scratch_shapes=[
            PARAMS,
            pltpu.VMEM((3, 3, 64, 128), F32),
            pltpu.VMEM((512, 2304), BF16),
            pltpu.VMEM((3, planes + 2, CY * channels, cells + 256), BF16),
            DMA((6,)),
        ],
        cost_estimate=pl.CostEstimate(flops=2 * 512 * 2304 * cells, bytes_accessed=8 << 20, transcendentals=0),
        compiler_params=SMALL,
        name="score",
    )(params, far(field), below, above, turned, values)

    final = pl.pallas_call(
        gradient_kernel,
        out_shape=jax.ShapeDtypeStruct((roles * devices * 8, 128), BF16),
        in_specs=[VMEM] * 7 + [HBM] * 3,
        out_specs=VMEM,
        scratch_shapes=[
            pltpu.VMEM((512, cells), BF16),
            pltpu.VMEM((512, 768), F32),
            pltpu.VMEM((512, 128), F32),
            pltpu.VMEM((64 * count, 1024), BF16),
            pltpu.VMEM((64 * count, 1024), BF16),
            pltpu.VMEM((3, planes, CY * channels, cells), BF16),
            DMA((11,)),
        ],
        cost_estimate=pl.CostEstimate(flops=2 * 512 * 768 * cells, bytes_accessed=8 << 20, transcendentals=0),
        compiler_params=SMALL,
        name="gradient",
    )(
        values,
        near(arrived.reshape(devices * SENT, 128)),
        near(hot), mr, inverse, mine_row, vec, far(g), far(u), far(field),
    )
    final = lax.all_to_all(
        final.reshape(roles * devices, 8, 128), ("role", "dev"), 0, 0, tiled=True
    )
    weight_grad, vector_grad = pl.pallas_call(
        finish_kernel,
        out_shape=(
            jax.ShapeDtypeStruct((1, 864), F32),
            jax.ShapeDtypeStruct((1, 3), F32),
        ),
        in_specs=[VMEM],
        out_specs=(VMEM, VMEM),
        compiler_params=SMALL,
        name="finish",
    )(near(final))
    return (scores.reshape(1, planes, height, columns), weight_grad, vector_grad)


def solution(mesh):
    in_specs = (
        P("role", None, "dev", None, None),
        P("role", "dev", None, None),
        P("role", None, None),
        P("dev", None),
        P("dev"),
        P("dev"),
        P("dev"),
        P("dev"),
        P("dev"),
    )
    out_specs = (P("role", "dev", None, None), P("dev", None), P("dev", None))
    return jax.shard_map(
        per_device, mesh=mesh, in_specs=in_specs, out_specs=out_specs, check_vma=False
    )
```

```python
import jax
import jax.numpy as jnp
from jax import lax
from jax.experimental import pallas as pl
from jax.experimental.pallas import tpu as pltpu
from jax.sharding import PartitionSpec as P


CY = 4
EPS = 1e-05
SENT = 48
F32 = jnp.float32
BF16 = jnp.bfloat16
PARAMS = pltpu.VMEM((512, 128), F32)
VMEM = pl.BlockSpec(memory_space=pltpu.VMEM)
SMALL = pltpu.CompilerParams(vmem_limit_bytes=20 << 20)
HBM = pl.BlockSpec(memory_space=pltpu.HBM)
DMA = pltpu.SemaphoreType.DMA
SMEM = pl.BlockSpec(memory_space=pltpu.SMEM)


def near(x):
    return pltpu.with_memory_space_constraint(x, pltpu.VMEM)


def far(x):
    return pltpu.with_memory_space_constraint(x, pltpu.HBM)


def lane_iota(rows=64):
    return lax.broadcasted_iota(jnp.int32, (rows, 128), 1)


def roll_lanes(x, shift):
    shift %= 128
    return x if shift == 0 else pltpu.roll(x, shift, 1)


def load_params(w_ref, p_ref):
    wide = w_ref[...].astype(F32)
    p_ref[...] = wide.reshape(wide.shape[0] * 8, 128)


def chunk(p_ref, k):
    return p_ref[pl.ds(k, 64, stride=8), :]


def column(v_ref, k):
    return v_ref[:, k : k + 1]


def fill_taps(p_ref, taps_ref):
    block = lane_iota() // 32
    chunks = [chunk(p_ref, k) for k in range(7)]
    for a in range(3):
        for c in range(3):
            out = jnp.zeros((64, 128), F32)
            for b in range(3):
                tap = 9 * a + 3 * b + c
                moved = roll_lanes(chunks[tap // 4], 32 * (b - tap % 4))
                out = jnp.where(block == b, moved, out)
            taps_ref[c, a] = out


def banded(taps_ref, c, a, yo):
    block = lane_iota() // 32
    v = roll_lanes(taps_ref[c, a], 32 * (yo - 1))
    if yo == 0:
        v = jnp.where(block == 3, 0.0, v)
    if yo == 3:
        v = jnp.where(block == 0, 0.0, v)
    return v


def pack_kernel(weight_ref, out_ref):
    sub = lax.broadcasted_iota(jnp.int32, (8, 128), 0)
    out = jnp.zeros((8, 128), F32)
    for k in range(6):
        out = jnp.where(sub == k, weight_ref[:, 128 * k : 128 * k + 128], out)
    tail = jnp.concatenate([weight_ref[:, 768:864], jnp.zeros((1, 32), F32)], axis=1)
    out = jnp.where(sub == 6, tail, out)
    out_ref[...] = jnp.broadcast_to(out.astype(BF16)[None], out_ref.shape)


def shifted(v):
    lane = lax.broadcasted_iota(jnp.int32, v.shape, 1)
    left = jnp.where(lane == 0, 0.0, pltpu.roll(v, 1, 1))
    right = jnp.where(lane == 127, 0.0, pltpu.roll(v, 127, 1))
    return left, v, right


def prep_kernel(slab_ref, x_ref, first_ref, last_ref, plane_ref, sem):
    channels, _, height, _ = slab_ref.shape
    to = lax.broadcasted_iota(jnp.int32, (256, 256), 0)
    source = lax.broadcasted_iota(jnp.int32, (256, 256), 1)
    exchange = (to // 16 == source % 16) & (to % 16 == source // 16)
    exchange = jnp.where(exchange, 1.0, 0.0).astype(BF16)
    for h in range(channels // 16):
        for g in range(height // 16):
            block = slab_ref[16 * h : 16 * h + 16, 0, 16 * g : 16 * g + 16, :]
            out = jnp.dot(exchange, block.reshape(256, 128), preferred_element_type=F32)
            for k in range(16):
                y = 16 * g + k
                v = out[16 * k : 16 * k + 16]
                rows = slice(32 * (y % CY) + 16 * h, 32 * (y % CY) + 16 * h + 16)
                lanes = slice(128 * (y // CY), 128 * (y // CY) + 128)
                for c, w in enumerate(shifted(v)):
                    x_ref[c, 0, rows, lanes] = w.astype(BF16)
                plane_ref[pl.program_id(0), rows, lanes] = v.astype(BF16)
    last = pl.num_programs(0) - 1
    first_copy = pltpu.make_async_copy(plane_ref.at[0], first_ref.at[0], sem.at[0])
    last_copy = pltpu.make_async_copy(plane_ref.at[last], last_ref.at[0], sem.at[1])

    @pl.when(pl.program_id(0) == 0)
    def _():
        first_copy.start()

    @pl.when(pl.program_id(0) == last)
    def _():
        last_copy.start()
        first_copy.wait()
        last_copy.wait()


def crop_conv_kernel(
    gain_ref, shift_ref, head_ref, mean_ref, var_ref, w_ref, x_ref, out_ref, stats_ref, p_ref, taps_ref, t_ref, s1_ref, m2_ref, u_ref, sem
):
    load_params(w_ref, p_ref)
    fill_taps(p_ref, taps_ref)
    for zo in range(2):
        for yo in range(4):
            row = 64 * (4 * zo + yo)
            for c in range(3):
                for z in range(2):
                    col = 256 * c + 128 * z
                    v = banded(taps_ref, c, z - zo + 1, yo)
                    t_ref[row : row + 64, col : col + 128] = v.astype(BF16)
    s1_ref[...] = jnp.zeros((64, 128), F32)
    m2_ref[...] = jnp.zeros((64, 128), F32)
    lanes = lane_iota()

    def convolve(p):
        dst = pl.multiple_of(256 * p, 128)
        x = jnp.concatenate(
            [x_ref[c, z, :, pl.ds(dst, 256)] for c in range(3) for z in range(2)], axis=0
        )
        u = jnp.dot(t_ref[...], x, preferred_element_type=F32).astype(BF16)
        for half in range(2):
            for j in range(8):
                u_ref[pl.ds(pl.multiple_of(64 * (2 * p + half), 64), 64), 128 * j : 128 * j + 128] = u[
                    64 * j : 64 * j + 64, 128 * half : 128 * half + 128
                ]

        leave(p).start()

    def leave(p):
        rows = pl.ds(pl.multiple_of(128 * p, 128), 128)
        return pltpu.make_async_copy(u_ref.at[rows], out_ref.at[rows], sem.at[p])

    def statistics(p, u):
        for half in range(2):
            parts = [
                u[64 * half : 64 * half + 64, 128 * j : 128 * j + 128].astype(F32)
                for j in range(8)
            ]
            total = jnp.sum(sum(parts), axis=1, keepdims=True)
            mean = total * (1.0 / 1024)
            square = jnp.zeros((64, 128), F32)
            for part in parts:
                d = part - mean
                square = square + d * d
            here = lanes == 2 * p + half
            s1_ref[...] = jnp.where(here, total, s1_ref[...])
            m2_ref[...] = jnp.where(here, jnp.sum(square, axis=1, keepdims=True), m2_ref[...])

    convolve(0)
    pairs = u_ref.shape[0] // 128
    for p in range(1, pairs):
        before = u_ref[128 * p - 128 : 128 * p, :]
        convolve(p)
        statistics(p - 1, before)
    statistics(pairs - 1, u_ref[128 * (pairs - 1) :, :])
    stat = jnp.concatenate([s1_ref[...], m2_ref[...]], axis=0).T[:16]
    low = lanes[:16] < 64
    high_term = stat.astype(BF16).astype(F32)
    top = jnp.where(low, high_term, pltpu.roll(stat - high_term, 64, 1))
    squares = jnp.where(low[:8], pltpu.roll(stat, 64, 1)[:8], stat[8:])
    sub = lax.broadcasted_iota(jnp.int32, (8, 128), 0)
    tail = jnp.zeros((8, 128), F32)
    for k, ref in enumerate((gain_ref, shift_ref, head_ref, mean_ref, var_ref)):
        tail = jnp.where((sub == 0) & (lanes[:8] == k), ref[0], tail)
    stats = jnp.concatenate([top, squares, tail], axis=0).astype(BF16)

    def spread(s, _):
        stats_ref[s] = stats
        return 0

    lax.fori_loop(0, stats_ref.shape[0], spread, 0, unroll=8)
    for p in range(8):
        leave(p).wait()


def score_kernel(
    w_ref, x_ref, below_ref, above_ref, cbt_ref, v_ref, out_ref, hot_ref, p_ref, taps_ref, t_ref, f_ref, sem
):
    count = x_ref.shape[3] // 128
    arrive = []
    for c in range(3):
        for z in range(2):
            inside = f_ref.at[c, 1 + z, :, pl.ds(128, 128 * count)]
            arrive.append(pltpu.make_async_copy(x_ref.at[c, z], inside, sem.at[2 * c + z]))
            arrive[-1].start()
    learners, sources = cbt_ref.shape
    entries = hot_ref.shape[1]
    live = jnp.where(cbt_ref[...] >= 0, 1.0, 0.0)
    earlier = lax.broadcasted_iota(jnp.int32, (learners, learners), 1) < lax.broadcasted_iota(
        jnp.int32, (learners, learners), 0
    )
    place = jnp.dot(
        jnp.where(earlier, 1.0, 0.0).astype(BF16), live.astype(BF16), preferred_element_type=F32
    )
    place = jnp.where(live > 0, place, -1.0).astype(BF16)
    lane = lax.broadcasted_iota(jnp.int32, (sources, entries), 1)
    start = SENT * lax.broadcasted_iota(jnp.int32, (sources, entries), 0)
    expand = jnp.where((lane >= start) & (lane < start + SENT), 1.0, 0.0).astype(BF16)
    wanted = jnp.dot(place, expand, preferred_element_type=F32)
    slot = (lax.broadcasted_iota(jnp.int32, (8, entries), 1) % SENT).astype(F32)[0:1]
    hot_ref[...] = jnp.where(wanted == slot, 1.0, 0.0).astype(BF16)
    load_params(w_ref, p_ref)
    fill_taps(p_ref, taps_ref)
    block = lane_iota() // 32
    zero = jnp.zeros((64, 128), F32)
    for zo in range(2):
        for yo in range(4):
            row = slice(64 * (4 * zo + yo), 64 * (4 * zo + yo) + 64)
            for c in range(3):
                edges = []
                for zz in range(4):
                    a = zz - zo
                    inside = 0 <= a <= 2
                    v = banded(taps_ref, c, a, yo) if inside else zero
                    col = 128 * (4 * c + zz)
                    t_ref[row, col : col + 128] = v.astype(BF16)
                    odd = zz % 2
                    if inside and yo == 0:
                        v = roll_lanes(taps_ref[c, a], 64 * odd)
                        edges.append(jnp.where(block == 2 * odd, v, 0.0))
                    elif inside and yo == 3:
                        v = roll_lanes(taps_ref[c, a], 64 * odd - 32)
                        edges.append(jnp.where(block == 2 * odd + 1, v, 0.0))
                    else:
                        edges.append(zero)
                for k in range(2):
                    col = 1536 + 128 * (2 * c + k)
                    v = edges[2 * k] + edges[2 * k + 1]
                    t_ref[row, col : col + 128] = v.astype(BF16)
    gain, shift, head, mean, var = (column(v_ref, k) for k in range(5))
    alpha = gain * lax.rsqrt(var + EPS)
    beta = shift - mean * alpha
    alpha = jnp.broadcast_to(alpha, (64, 128))
    beta = jnp.broadcast_to(beta, (64, 128))
    head = jnp.broadcast_to(head, (64, 128))

    empty = jnp.zeros((128, 128), BF16)
    for c in range(3):
        for zz in range(4):
            f_ref[c, zz, :, 0:128] = empty
            f_ref[c, zz, :, 128 * (count + 1) : 128 * (count + 2)] = empty

    def halo(b, _):
        src = pl.multiple_of(128 * b, 128)
        dst = pl.multiple_of(128 * b + 128, 128)
        for zz, ref in ((0, below_ref), (3, above_ref)):
            v = ref[0, :, pl.ds(src, 128)].astype(F32)
            for c, w in enumerate(shifted(v)):
                f_ref[c, zz, :, pl.ds(dst, 128)] = w.astype(BF16)
        return 0

    lax.fori_loop(0, count, halo, 0)
    for copy in arrive:
        copy.wait()

    def step(p, _):
        at = pl.multiple_of(256 * p, 128)
        pairs = [(c, zz) for c in range(3) for zz in range(4)]
        rows = [f_ref[c, zz, :, pl.ds(at + 128, 256)] for c, zz in pairs]
        for c, zz in pairs:
            rows.append(f_ref[c, zz, 96:128, pl.ds(at, 256)])
            rows.append(f_ref[c, zz, 0:32, pl.ds(at + 256, 256)])
        out = jnp.dot(t_ref[...], jnp.concatenate(rows, axis=0), preferred_element_type=F32)
        for half in range(2):
            for j in range(8):
                v = out[64 * j : 64 * j + 64, 128 * half : 128 * half + 128]
                h = jnp.maximum(v * alpha + beta, 0.0) * head
                out_ref[j // 4, 2 * p + half, j % 4 : j % 4 + 1, :] = jnp.sum(
                    h, axis=0, keepdims=True
                )
        return 0

    lax.fori_loop(0, count // 2, step, 0)


def exact_dot(a, v):
    hi = v.astype(BF16)
    rest = v - hi.astype(F32)
    mid = rest.astype(BF16)
    low = (rest - mid.astype(F32)).astype(BF16)
    out = jnp.dot(a, low, preferred_element_type=F32)
    out = out + jnp.dot(a, mid, preferred_element_type=F32)
    return out + jnp.dot(a, hi, preferred_element_type=F32)


def learner_kernel(
    cb_ref, r_ref, table_ref, u_in_ref, given_ref,
    send_out_ref, g_out_ref, mr_ref, vec_ref, inv_ref, row_ref, v_ref, cbt_ref,
    p_ref, acc_ref, part_ref, coef_ref, scale_ref, al_ref, be_ref, hd_ref, r0_ref, ru_ref,
    u_ref, send_ref, g_ref, lab_ref, sem,
):
    arrive = pltpu.make_async_copy(u_in_ref, u_ref, sem.at[0])
    arrive.start()
    cbt_ref[...] = table_ref[...].astype(F32).T
    given = given_ref[...].astype(F32)
    for b in range(lab_ref.shape[0]):
        lab_ref[b] = jnp.concatenate([given[z, CY * b : CY * b + CY] for z in range(2)], axis=0)
    lanes = lane_iota()
    learners, sources = cbt_ref.shape
    entries = sources * 16
    lane = lax.broadcasted_iota(jnp.int32, (sources, entries), 1)
    source = lax.broadcasted_iota(jnp.int32, (sources, entries), 0)
    expand = jnp.where(lane // 16 == source, 1.0, 0.0).astype(BF16)
    wanted = jnp.dot(cbt_ref[...].astype(BF16), expand, preferred_element_type=F32)
    which = lax.broadcasted_iota(jnp.int32, (learners, entries), 1) % 16
    onehot = jnp.where(wanted == which.astype(F32), 1.0, 0.0).astype(BF16)
    number = jnp.sum(jnp.where(cbt_ref[...] >= 0, 1.0, 0.0), axis=1, keepdims=True)
    wide = r_ref[...].astype(F32)
    low_half = lax.broadcasted_iota(jnp.int32, (entries, 128), 1) < 64
    top = wide[:, :16].reshape(entries, 128)
    squares = wide[:, 16:24]
    swapped = pltpu.roll(squares.reshape(sources * 8, 128), 64, 1).reshape(sources, 8, 128)
    squares = jnp.concatenate([swapped, squares], axis=1).reshape(entries, 128)
    r = jnp.where(low_half, top + pltpu.roll(top, 64, 1), squares)
    p_ref[...] = wide[:, 24:32].reshape(sources * 8, 128)
    v_ref[...] = p_ref[pl.ds(0, sources, stride=8), :]
    means = r * (1.0 / 1024)
    centre = jnp.mean(means, axis=0, keepdims=True)
    d = means - centre
    rolled = pltpu.roll(d, 64, 1)
    v = jnp.where(low_half, d, means + rolled * rolled)
    p = exact_dot(onehot, v) / number
    first = jnp.where(lanes < 64, p, 0.0)
    mu = first + centre
    var = pltpu.roll(p, 64, 1) - first * first
    rstd = lax.rsqrt(jnp.maximum(var, 0.0) + EPS)
    both = jnp.where(lanes < 64, mu, pltpu.roll(rstd, 64, 1))
    both_t = jnp.concatenate([both, jnp.zeros((128 - learners, 128), F32)], axis=0).T
    mr_ref[...] = both_t
    inverse = jnp.broadcast_to(1.0 / (number * 1024.0), (learners, 128))
    inverse = jnp.concatenate([inverse, jnp.zeros((128 - learners, 128), F32)], axis=0).T
    inv_ref[...] = inverse[:8]
    row_ref[...] = jnp.full((8, 128), -1, jnp.int32)
    gain, shift, head = (jnp.broadcast_to(column(v_ref, k), (64, 128)) for k in range(3))
    alpha = gain * both_t[64:]
    al_ref[...] = alpha
    be_ref[...] = shift - alpha * both_t[:64]
    hd_ref[...] = head
    r0_ref[...] = jnp.zeros((64, 128), F32)
    ru_ref[...] = jnp.zeros((64, 128), F32)
    zero = jnp.minimum(jnp.maximum(p[0:1], 0.0), 0.0)
    zero = jnp.broadcast_to(zero, (64, 128))
    for j in range(8):
        for b in range(acc_ref.shape[0] // 64):
            acc_ref[64 * b : 64 * b + 64, 128 * j : 128 * j + 128] = zero
    part_ref[...] = jnp.zeros_like(part_ref)
    live = cb_ref[2 * learners]
    arrive.wait()

    def reduce(k, e):
        here = lanes == k
        r0 = jnp.sum(part_ref[2 * e], axis=1, keepdims=True)
        rh = jnp.sum(part_ref[2 * e + 1], axis=1, keepdims=True)
        r0_ref[...] = jnp.where(here, r0, r0_ref[...])
        ru_ref[...] = jnp.where(here, rh, ru_ref[...])

    def fetch(k):
        t = cb_ref[jnp.minimum(k, live - 1)]
        index = jnp.full((64, 128), t, jnp.int32)
        inv = jnp.take_along_axis(inv_ref[...], index[:8], axis=1)
        al = jnp.take_along_axis(al_ref[...], index, axis=1)
        be = jnp.take_along_axis(be_ref[...], index, axis=1)
        return jnp.where(k < live, inv, 0.0), al, be, hd_ref[...] * al

    def keep(e, coefficients):
        scale_ref[e] = coefficients[0]
        for n in range(3):
            coef_ref[3 * e + n] = coefficients[1 + n]

    def learner(k, e):
        t = cb_ref[jnp.minimum(k, live - 1)]
        b = cb_ref[learners + t]
        row = pl.multiple_of(b * 64, 64)
        row_ref[...] = jnp.where(lanes[:8] == t, b, row_ref[...])
        al, be, c1 = (coef_ref[3 * e + n] for n in range(3))
        inv = scale_ref[e, 0:1]
        hd = hd_ref[...]
        r0 = jnp.zeros((64, 128), F32)
        rh = jnp.zeros((64, 128), F32)
        for j in range(8):
            us = u_ref[pl.ds(row, 64), 128 * j : 128 * j + 128].astype(F32)
            h = jnp.maximum(us * al + be, 0.0)
            score = jnp.sum(h * hd, axis=0, keepdims=True)
            res = (score - lab_ref[b, j : j + 1, :]) * inv
            m = jnp.where(h > 0, res, 0.0)
            r0 = r0 + m
            rh = rh + h * res
            acc_ref[pl.ds(row, 64), 128 * j : 128 * j + 128] += c1 * m
        part_ref[2 * e] = r0
        part_ref[2 * e + 1] = rh

    def step(i, _):
        for e in range(2):
            reduce(2 * i - 2 + e, e)
        following = [fetch(2 * i + 2 + e) for e in range(2)]
        for e in range(2):
            learner(2 * i + e, e)
            keep(e, following[e])
        return 0

    for e in range(2):
        keep(e, fetch(e))
    steps = (live + 1) // 2
    lax.fori_loop(0, steps, step, 0)
    leaves = []
    for j in range(8):
        rows = slice(128 * j, 128 * j + 128)
        g_ref[rows, :] = acc_ref[rows, :].astype(BF16)
        leaves.append(pltpu.make_async_copy(g_ref.at[rows], g_out_ref.at[rows], sem.at[2 + j]))
        leaves[j].start()
    for e in range(2):
        reduce(2 * steps - 2 + e, e)
    r0 = r0_ref[...]
    r1 = (ru_ref[...] - shift * r0) / gain
    sends = send_ref.shape[1]
    out = jnp.concatenate([r0, r1], axis=0).T[:sends].astype(BF16)

    def spread(s, _):
        send_ref[s] = out
        return 0

    lax.fori_loop(0, send_ref.shape[0], spread, 0, unroll=8)
    send = pltpu.make_async_copy(send_ref, send_out_ref, sem.at[1])
    send.start()
    dgain = jnp.sum(head * r1, axis=1, keepdims=True)
    dshift = jnp.sum(head * r0, axis=1, keepdims=True)
    dhead = jnp.sum(gain * r1 + shift * r0, axis=1, keepdims=True)
    vec_ref[...] = jnp.where(
        lanes == 96, dgain, jnp.where(lanes == 97, dshift, jnp.where(lanes == 98, dhead, 0.0))
    )
    send.wait()
    for leave in leaves:
        leave.wait()


def gradient_kernel(
    v_ref, r_ref, hot_ref, mr_ref, inv_ref, cb_ref, vec_ref, g_in_ref, u_in_ref, x_in_ref,
    out_ref, full_ref, dt_ref, row_ref, g_ref, u_ref, x_ref, sem,
):
    arrive = []
    for q in range(4):
        rows = pl.ds(256 * q, 256)
        arrive.append(pltpu.make_async_copy(g_in_ref.at[rows], g_ref.at[rows], sem.at[2 * q]))
        arrive.append(pltpu.make_async_copy(u_in_ref.at[rows], u_ref.at[rows], sem.at[2 * q + 1]))
    arrive += [pltpu.make_async_copy(x_in_ref.at[c], x_ref.at[c], sem.at[8 + c]) for c in range(3)]
    for copy in arrive:
        copy.start()
    learners = hot_ref.shape[0]
    total = jnp.dot(hot_ref[...], r_ref[...], preferred_element_type=F32)
    total = jnp.concatenate([total, jnp.zeros((128 - learners, 128), F32)], axis=0).T
    gain, head = (jnp.broadcast_to(column(v_ref, k), (64, 128)) for k in (0, 2))
    factor = gain * head * inv_ref[0:1, :]
    first = factor * total[:64]
    second = factor * total[64:]
    mu = mr_ref[:64]
    rstd = mr_ref[64:]
    slope = rstd * rstd * second
    offset = rstd * first - slope * mu
    row = cb_ref[0:1, :]

    def block(b, _):
        at = pl.multiple_of(b * 128, 128)
        row64 = pl.multiple_of(b * 64, 64)
        here = row == b
        e = jnp.broadcast_to(jnp.sum(jnp.where(here, offset, 0.0), axis=1, keepdims=True), (64, 128))
        f = jnp.broadcast_to(jnp.sum(jnp.where(here, slope, 0.0), axis=1, keepdims=True), (64, 128))
        for j in range(8):
            rows = slice(64 * j, 64 * j + 64)
            v = g_ref[pl.ds(row64, 64), 128 * j : 128 * j + 128].astype(F32) - e
            v = v - f * u_ref[pl.ds(row64, 64), 128 * j : 128 * j + 128].astype(F32)
            full_ref[rows, pl.ds(at, 128)] = v.astype(BF16)
        return 0

    for q in range(4):
        arrive[2 * q].wait()
        arrive[2 * q + 1].wait()
        lax.fori_loop(4 * q, 4 * q + 4, block, 0, unroll=4)
    for c in range(3):
        arrive[8 + c].wait()
        dt_ref[:, 256 * c : 256 * c + 256] = lax.dot_general(
            full_ref[...],
            jnp.concatenate([x_ref[c, 0], x_ref[c, 1]], axis=0),
            (((1,), (1,)), ((), ())),
            preferred_element_type=F32,
        )
    blocks = lane_iota() // 32
    outs = [jnp.zeros((64, 128), F32) for _ in range(6)] + [vec_ref[...]]
    for c in range(3):
        for a in range(3):
            acc = jnp.zeros((64, 128), F32)
            for zo in range(2):
                z = zo + a - 1
                if not 0 <= z <= 1:
                    continue
                for yo in range(4):
                    j = 4 * zo + yo
                    col = 256 * c + 128 * z
                    v = roll_lanes(dt_ref[64 * j : 64 * j + 64, col : col + 128], -32 * (yo - 1))
                    if yo == 0:
                        v = jnp.where(blocks == 0, 0.0, v)
                    if yo == 3:
                        v = jnp.where(blocks == 2, 0.0, v)
                    acc = acc + v
            for b in range(3):
                tap = 9 * a + 3 * b + c
                k = tap // 4
                outs[k] = jnp.where(
                    blocks == tap % 4, roll_lanes(acc, 32 * (tap % 4 - b)), outs[k]
                )
    outs.append(jnp.zeros((64, 128), F32))
    for k in range(8):
        row_ref[pl.ds(k, 64, stride=8), :] = outs[k]
    packed = row_ref[...].astype(BF16)
    for role in range(out_ref.shape[0] // 512):
        out_ref[512 * role : 512 * role + 512, :] = packed


def finish_kernel(r_ref, weight_ref, vector_ref):
    total = jnp.sum(r_ref[...].astype(F32), axis=0)
    for k in range(6):
        weight_ref[:, 128 * k : 128 * k + 128] = total[k : k + 1]
    weight_ref[:, 768:864] = total[6:7, :96]
    vector_ref[...] = total[6:7, 96:99]


def per_device(features, labels, crop_block, weight, gain, shift, head, run_mean, run_var):
    devices = lax.axis_size("dev")
    roles = lax.axis_size("role")
    rows = pl.pallas_call(
        pack_kernel,
        out_shape=jax.ShapeDtypeStruct((devices, 8, 128), BF16),
        in_specs=[VMEM],
        out_specs=VMEM,
        compiler_params=SMALL,
        name="pack",
    )(far(weight))
    params = near(lax.all_to_all(rows, "dev", 0, 0, tiled=True))

    slab = features[0]
    channels, planes, height, columns = slab.shape
    count = height // CY
    cells = count * columns
    field, first, last = pl.pallas_call(
        prep_kernel,
        out_shape=(
            pltpu.VMEM((3, planes, CY * channels, cells), BF16),
            pltpu.HBM((1, CY * channels, cells), BF16),
            pltpu.HBM((1, CY * channels, cells), BF16),
        ),
        grid=(planes,),
        in_specs=[pl.BlockSpec((channels, 1, height, columns), lambda z: (0, z, 0, 0))],
        out_specs=(
            pl.BlockSpec((3, 1, CY * channels, cells), lambda z: (0, z, 0, 0)),
            HBM,
            HBM,
        ),
        scratch_shapes=[
            pltpu.VMEM((planes, CY * channels, cells), BF16),
            DMA((2,)),
        ],
        cost_estimate=pl.CostEstimate(flops=10**7, bytes_accessed=4 << 20, transcendentals=0),
        compiler_params=SMALL,
        name="prep",
    )(far(slab))

    *vectors, _ = lax.optimization_barrier((gain, shift, head, run_mean, run_var, field))
    u, stats = pl.pallas_call(
        crop_conv_kernel,
        out_shape=(
            pltpu.HBM((64 * count, 1024), BF16),
            pltpu.HBM((devices, 32, 128), BF16),
        ),
        in_specs=[SMEM] * 5 + [VMEM] * 2,
        out_specs=(HBM, VMEM),
        scratch_shapes=[
            PARAMS,
            pltpu.VMEM((3, 3, 64, 128), F32),
            pltpu.VMEM((512, 768), BF16),
            pltpu.VMEM((64, 128), F32),
            pltpu.VMEM((64, 128), F32),
            pltpu.VMEM((64 * count, 1024), BF16),
            DMA((8,)),
        ],
        cost_estimate=pl.CostEstimate(flops=2 * 512 * 768 * cells, bytes_accessed=8 << 20, transcendentals=0),
        compiler_params=SMALL,
        name="crop_conv",
    )(*vectors, params, near(field))

    table, _ = lax.optimization_barrier((crop_block[0], stats))
    own_index = lax.axis_index("dev")
    mine = lax.dynamic_slice_in_dim(table, own_index, 1, 0)[0]
    live = mine >= 0
    places = jnp.arange(devices)
    before = jnp.sum(live[None, :] & (places[None, :] < places[:, None]), axis=1)
    at = live[None, :] & (before[None, :] == places[:, None])
    order = jnp.sum(jnp.where(at, places[None, :], 0), axis=1)
    lists = jnp.concatenate([order, mine, jnp.sum(live.astype(jnp.int32))[None]]).astype(jnp.int32)
    gathered = lax.all_to_all(stats, "dev", 0, 0, tiled=True)
    below = lax.ppermute(last, "dev", [(i, i + 1) for i in range(devices - 1)])
    above = lax.ppermute(first, "dev", [(i + 1, i) for i in range(devices - 1)])

    send, g, mr, vec, inverse, mine_row, values, turned = pl.pallas_call(
        learner_kernel,
        out_shape=(
            pltpu.HBM((devices, SENT, 128), BF16),
            pltpu.HBM((64 * count, 1024), BF16),
            jax.ShapeDtypeStruct((128, 128), F32),
            jax.ShapeDtypeStruct((64, 128), F32),
            jax.ShapeDtypeStruct((8, 128), F32),
            jax.ShapeDtypeStruct((8, 128), jnp.int32),
            jax.ShapeDtypeStruct((64, 128), F32),
            jax.ShapeDtypeStruct((devices, devices), F32),
        ),
        in_specs=[SMEM] + [VMEM] * 2 + [HBM, VMEM],
        out_specs=(HBM, HBM) + (VMEM,) * 6,
        scratch_shapes=[
            PARAMS,
            pltpu.VMEM((64 * count, 1024), F32),
            pltpu.VMEM((4, 64, 128), F32),
            pltpu.VMEM((6, 64, 128), F32),
            pltpu.VMEM((2, 8, 128), F32),
        ]
        + [pltpu.VMEM((64, 128), F32)] * 5
        + [
            pltpu.VMEM((64 * count, 1024), BF16),
            pltpu.VMEM((devices, SENT, 128), BF16),
            pltpu.VMEM((64 * count, 1024), BF16),
            pltpu.VMEM((count, planes * CY, columns), F32),
            DMA((10,)),
        ],
        cost_estimate=pl.CostEstimate(flops=10**10, bytes_accessed=8 << 20, transcendentals=0),
        compiler_params=SMALL,
        name="learner",
    )(lists, near(gathered), table, far(u), labels[0])

    arrived = lax.all_to_all(send, "dev", 0, 0, tiled=True)

    scores, hot = pl.pallas_call(
        score_kernel,
        out_shape=(
            jax.ShapeDtypeStruct((planes, count, CY, columns), F32),
            pltpu.VMEM((devices, devices * SENT), BF16),
        ),
        in_specs=[VMEM, HBM] + [VMEM] * 4,
        out_specs=(VMEM, VMEM),
        scratch_shapes=[
            PARAMS,
            pltpu.VMEM((3, 3, 64, 128), F32),
            pltpu.VMEM((512, 2304), BF16),
            pltpu.VMEM((3, planes + 2, CY * channels, cells + 256), BF16),
            DMA((6,)),
        ],
        cost_estimate=pl.CostEstimate(flops=2 * 512 * 2304 * cells, bytes_accessed=8 << 20, transcendentals=0),
        compiler_params=SMALL,
        name="score",
    )(params, far(field), below, above, turned, values)

    final = pl.pallas_call(
        gradient_kernel,
        out_shape=jax.ShapeDtypeStruct((roles * devices * 8, 128), BF16),
        in_specs=[VMEM] * 7 + [HBM] * 3,
        out_specs=VMEM,
        scratch_shapes=[
            pltpu.VMEM((512, cells), BF16),
            pltpu.VMEM((512, 768), F32),
            pltpu.VMEM((512, 128), F32),
            pltpu.VMEM((64 * count, 1024), BF16),
            pltpu.VMEM((64 * count, 1024), BF16),
            pltpu.VMEM((3, planes, CY * channels, cells), BF16),
            DMA((11,)),
        ],
        cost_estimate=pl.CostEstimate(flops=2 * 512 * 768 * cells, bytes_accessed=8 << 20, transcendentals=0),
        compiler_params=SMALL,
        name="gradient",
    )(
        values,
        near(arrived.reshape(devices * SENT, 128)),
        near(hot), mr, inverse, mine_row, vec, far(g), far(u), far(field),
    )
    final = lax.all_to_all(
        final.reshape(roles * devices, 8, 128), ("role", "dev"), 0, 0, tiled=True
    )
    weight_grad, vector_grad = pl.pallas_call(
        finish_kernel,
        out_shape=(
            jax.ShapeDtypeStruct((1, 864), F32),
            jax.ShapeDtypeStruct((1, 3), F32),
        ),
        in_specs=[VMEM],
        out_specs=(VMEM, VMEM),
        compiler_params=SMALL,
        name="finish",
    )(near(final))
    return (scores.reshape(1, planes, height, columns), weight_grad, vector_grad)


def solution(mesh):
    in_specs = (
        P("role", None, "dev", None, None),
        P("role", "dev", None, None),
        P("role", None, None),
        P("dev", None),
        P("dev"),
        P("dev"),
        P("dev"),
        P("dev"),
        P("dev"),
    )
    out_specs = (P("role", "dev", None, None), P("dev", None), P("dev", None))
    return jax.shard_map(
        per_device, mesh=mesh, in_specs=in_specs, out_specs=out_specs, check_vma=False
    )
```
